128 devices in a mesh: row: 8 (over x, core), col: 16 (over y, z).
Axes of the slice: x: 4, y: 4, z: 4, core: 2. Of those that a mesh axis runs over, the one named last changes fastest.
Arguments:
- hidden_states: bfloat16 [16384, 3072], P(('row', 'col')), may hold values from -27 to 27
- norm_gain: float32 [3072], replicated, may hold values from 0.25 to 1.75
- gate_base: bfloat16 [3072, 8192], P('row', 'col'), may hold values from -0.109375 to 0.109375
- up_base: bfloat16 [3072, 8192], P('row', 'col'), may hold values from -0.109375 to 0.109375
- down_base: bfloat16 [8192, 3072], P('col', 'row'), may hold values from -0.0625 to 0.0625
- shrink_gu: bfloat16 [2048, 3072], P('col'), may hold values from -0.109375 to 0.109375
- expand_gu: bfloat16 [2, 1024, 8192], P(None, None, 'col'), may hold values from -1.5 to 1.5
- down_shrink_maps: bfloat16 [1024, 8192], P(None, 'col'), may hold values from -0.0625 to 0.0625
- down_expand_maps: bfloat16 [1024, 3072], P('col'), may hold values from -1.5 to 1.5
- token_adapter: int32 [16384], P('row'), may hold values from 0 to 63, as said below
- adapter_slot: int32 [64], replicated, may hold values from 0 to 63, as said below
Outputs:
- mlp_out: bfloat16 [16384, 3072], P(('row', 'col'))
The draws below stay inside these ranges and needn't reach their ends.
Inputs may be any that keep to these rules, and one draw needn't show every extreme that they name: `token_adapter`: split the tokens into aligned blocks of 128 and groups of 16 consecutive blocks: no block has more than 16 tokens whose adapters share one owner, and in each group one owner has exactly 16 tokens in every block. `adapter_slot`: A permutation of the slots.
All inputs are finite; a program needn't handle non-finite values.
Results may differ from the reference program's by a relative error of at most 0.017.
Values may be sent and summed in bfloat16 or wider, within the bound.
No kernel may reach another device: no remote copies, remote signals or barrier semaphores. Data moves between devices by JAX's collectives and lax.ppermute only.
A program may use at most 128 MiB of HBM per device.

```python
import math
import jax
import jax.numpy as jnp
from jax import lax

D = 3072
FF = 8192
RANK = 16
ADAPT_DEV = 4
TOK_DEV = 128
CAP = 16
OWNERS = 16
ADAPTERS = 64
ROW_TOK = 2048
TOKENS = 16384
N_ROW = 8


def slot_table(key):
    return jax.random.permutation(jax.random.fold_in(key, 101), ADAPTERS).astype(jnp.int32)


def draw_adapter_slot(key, part):
    return slot_table(key)


def draw_token_adapter(key, part):
    slot_map = slot_table(key)
    holder = jnp.argsort(slot_map).astype(jnp.int32)
    blocks = TOKENS // TOK_DEV
    groups = blocks // OWNERS
    hot_owner = jax.random.randint(jax.random.fold_in(key, 102), (groups,), 0, OWNERS)
    hot_owner = jnp.repeat(hot_owner, OWNERS)
    offset = jax.random.randint(jax.random.fold_in(key, 103), (blocks,), 0, OWNERS - 1)
    position = jnp.arange(TOK_DEV, dtype=jnp.int32)
    others = (hot_owner[:, None] + 1 + (position[None, :] + offset[:, None]) % (OWNERS - 1)) % OWNERS
    owner_of = jnp.where(position[None, :] < CAP, hot_owner[:, None], others)
    block_keys = jax.random.split(jax.random.fold_in(key, 104), blocks)
    shuffle = jax.vmap(lambda one_key: jax.random.permutation(one_key, TOK_DEV))(block_keys)
    owner_of = jnp.take_along_axis(owner_of, shuffle, axis=1)
    local_index = jax.random.randint(jax.random.fold_in(key, 105), (blocks, TOK_DEV), 0, ADAPT_DEV)
    return holder[owner_of * ADAPT_DEV + local_index].reshape(TOKENS).astype(jnp.int32)


def draw_hidden_states(key, part):
    key_base = jax.random.fold_in(key, 1)
    key_rows = jax.random.fold_in(key, 2)
    key_cols = jax.random.fold_in(key, 3)
    values = jnp.clip(jax.random.normal(key_base, (TOKENS, D), jnp.float32), -3.0, 3.0)
    row_scale = jnp.exp(jax.random.uniform(key_rows, (TOKENS, 1), jnp.float32, math.log(0.3), math.log(3.0)))
    col_scale = jnp.exp(jax.random.uniform(key_cols, (1, D), jnp.float32, math.log(0.3), math.log(3.0)))
    return (values * row_scale * col_scale).astype(jnp.bfloat16)


def steps_of(stream_key, shape, cuts, smallest, largest):
    gain = 1.0
    for axis_at, parts in cuts:
        draws = jax.random.uniform(jax.random.fold_in(jax.random.fold_in(stream_key, 6), axis_at), (parts,), jnp.float32, smallest / len(cuts), largest / len(cuts))
        gain = gain * jnp.repeat(jnp.exp(draws), shape[axis_at] // parts).reshape((-1,) + (1,) * (len(shape) - 1 - axis_at))
    return gain


def gaussian(own_key, extent, width, most, cuts=(), held_as=jnp.bfloat16):
    array = width * jax.random.normal(own_key, extent, jnp.float32)
    if cuts:
        array = array * steps_of(own_key, extent, cuts, -0.22, 0.18)
    return jnp.clip(array, -most, most).astype(held_as)


def setup_inputs(seed: int = 0) -> dict:
    arg_keys = jax.random.split(jax.random.key(seed), 12)
    hidden_states = draw_hidden_states(jax.random.fold_in(arg_keys[11], 71), 0)
    norm_gain = jnp.clip(1.0 + 0.15 * jax.random.normal(arg_keys[1], (D,), jnp.float32), 0.25, 1.75)
    gate_base = gaussian(arg_keys[2], (D, FF), D ** -0.5, 0.109375, ((0, 8), (1, 16)))
    up_base = gaussian(arg_keys[3], (D, FF), D ** -0.5, 0.109375, ((0, 8), (1, 16)))
    down_base = gaussian(arg_keys[4], (FF, D), FF ** -0.5, 0.0625, ((0, 16), (1, 8)))
    shrink_gu = gaussian(arg_keys[5], (ADAPTERS * 2 * RANK, D), D ** -0.5, 0.109375, ((0, 16),))
    expand_gu = gaussian(arg_keys[6], (2, ADAPTERS * RANK, FF), RANK ** -0.5, 1.5, ((2, 16),))
    down_shrink_maps = gaussian(arg_keys[7], (ADAPTERS * RANK, FF), FF ** -0.5, 0.0625, ((1, 16),))
    down_expand_maps = gaussian(arg_keys[8], (ADAPTERS * RANK, D), RANK ** -0.5, 1.5, ((0, 16),))
    token_adapter = draw_token_adapter(jax.random.fold_in(arg_keys[11], 71), 0)
    adapter_slot = draw_adapter_slot(jax.random.fold_in(arg_keys[11], 71), 0)
    return {"hidden_states": hidden_states, "norm_gain": norm_gain, "gate_base": gate_base, "up_base": up_base, "down_base": down_base, "shrink_gu": shrink_gu, "expand_gu": expand_gu, "down_shrink_maps": down_shrink_maps, "down_expand_maps": down_expand_maps, "token_adapter": token_adapter, "adapter_slot": adapter_slot}


eps = 1e-05

def reference(hidden_states, norm_gain, gate_base, up_base, down_base, shrink_gu, expand_gu, down_shrink_maps, down_expand_maps, token_adapter, adapter_slot):
    block_width = FF // OWNERS
    adapter_range = jnp.arange(ADAPTERS, dtype=jnp.int32)
    matches = (token_adapter[:, None] == adapter_range[None, :]).astype(jnp.int32)
    slot_ids = lax.optimization_barrier(jnp.sum(matches * adapter_slot[None, :], axis=1)).astype(jnp.int32)
    down_blocks = down_base.reshape(OWNERS, block_width, D)

    def one_block(pieces):
        states, block_slots = pieces
        values = states.astype(jnp.float32)
        scale_inv = lax.rsqrt(lax.optimization_barrier(jnp.mean(values * values, axis=-1, keepdims=True)) + eps)
        normed = (values * scale_inv * norm_gain).astype(jnp.bfloat16)
        select_mask = (block_slots[:, None] == adapter_range[None, :]).astype(jnp.float32)
        select_bf = select_mask.astype(jnp.bfloat16)
        row_total = states.shape[0]
        projected_rows = jnp.dot(normed, shrink_gu.T, preferred_element_type=jnp.float32).reshape(row_total, ADAPTERS, 2 * RANK)
        ranks_gu = lax.optimization_barrier(jnp.sum(projected_rows * select_mask[:, :, None], axis=1)).astype(jnp.bfloat16)

        def spread_rank_rows(factors):
            return (select_bf[:, :, None] * factors[:, None, :]).reshape(row_total, ADAPTERS * RANK)
        gate_sum = jnp.dot(normed, gate_base, preferred_element_type=jnp.float32) + jnp.dot(spread_rank_rows(ranks_gu[:, :RANK]), expand_gu[0], preferred_element_type=jnp.float32)
        up_sum = jnp.dot(normed, up_base, preferred_element_type=jnp.float32) + jnp.dot(spread_rank_rows(ranks_gu[:, RANK:]), expand_gu[1], preferred_element_type=jnp.float32)
        hidden_rows = (jax.nn.silu(gate_sum) * up_sum).astype(jnp.bfloat16)
        down_projector = jnp.dot(hidden_rows, down_shrink_maps.T, preferred_element_type=jnp.float32).reshape(row_total, ADAPTERS, RANK)
        down_rank_rows = lax.optimization_barrier(jnp.sum(down_projector * select_mask[:, :, None], axis=1)).astype(jnp.bfloat16)
        adapter_down_term = jnp.dot(spread_rank_rows(down_rank_rows), down_expand_maps, preferred_element_type=jnp.float32).astype(jnp.bfloat16)
        adapter_down_term = lax.optimization_barrier(adapter_down_term).astype(jnp.float32)
        hidden_blocks = jnp.transpose(hidden_rows.reshape(row_total, OWNERS, block_width), (1, 0, 2))

        def add_block(running, block_pair):
            term = jnp.dot(block_pair[0], block_pair[1], preferred_element_type=jnp.float32).astype(jnp.bfloat16)
            term = lax.optimization_barrier(term).astype(jnp.float32)
            return (running + term, None)
        down_weight_shared, unused = lax.scan(add_block, jnp.zeros((row_total, D), jnp.float32), (hidden_blocks, down_blocks))
        return (down_weight_shared + adapter_down_term).astype(jnp.bfloat16)
    outputs = lax.map(one_block, (hidden_states.reshape(N_ROW, ROW_TOK, D), slot_ids.reshape(N_ROW, ROW_TOK)))
    return outputs.reshape(TOKENS, D)
```

```python
import jax
import jax.numpy as jnp
from jax import lax
from jax.sharding import Mesh, PartitionSpec as P

eps = 1e-05
ALL = ("x", "c", "y", "h", "l")
GROUP = ("c", "y", "l")

SOURCE = (0, 0, 0, 1, 1, 2, 4)
STEPS = (
    (("y", -1), ("y", 1), ("l", 1), ("y", -1), ("l", 1), ("l", 1), ("l", 1)),
    (("l", 1), ("y", 1), ("y", -1), ("y", 1), ("y", -1), ("y", 1), ("y", 1)),
)
BLOCK_Y = ((0, 1, -1, 0, 2, 1, -1, 2), (0, 0, -1, 1, -1, 1, 2, 2))
BLOCK_L = ((0, 0, 0, 1, 0, 1, 1, 1), (0, 1, 0, 0, 1, 1, 0, 1))
X_ORDER = (0, -1, 1, 2)


def flat(x, c, y, z):
    return (((x % 4) * 2 + c % 2) * 4 + y % 4) * 4 + z % 4


def pairs_of(move):
    return [
        (flat(x, c, y, z), flat(*move(x, c, y, z)))
        for x in range(4)
        for c in range(2)
        for y in range(4)
        for z in range(4)
    ]


def tree_pairs(k):
    def move(x, c, y, z):
        axis, shift = STEPS[c][k]
        return (x, c, y + shift, z) if axis == "y" else (x, c, y, z ^ 1)

    return pairs_of(move)


TREE = [tree_pairs(k) for k in range(7)]
TREE_BACK = [[(b, a) for a, b in pairs] for pairs in TREE]
CORE = pairs_of(lambda x, c, y, z: (x, 1 - c, y, z))
SAME_ROLE = pairs_of(lambda x, c, y, z: (x, c, y, z if c == 0 else 3 - z))
OTHER_ROLE = pairs_of(lambda x, c, y, z: (x, 1 - c, y, 3 - z if c == 0 else z))
X_UP = pairs_of(lambda x, c, y, z: (x + 1, c, y, z))
X_DOWN = pairs_of(lambda x, c, y, z: (x - 1, c, y, z))


def send(value, pairs):
    return lax.ppermute(value, ALL, pairs)


def contract_trailing(left, right):
    return lax.dot_general(
        left, right, (((left.ndim - 1,), (1,)), ((), ())), preferred_element_type=jnp.float32
    )


def dot(left, right):
    return jnp.dot(left, right, preferred_element_type=jnp.float32)


def rms_normed(states, norm_gain):
    values = states.astype(jnp.float32)
    scale_inv = lax.rsqrt(jnp.mean(values * values, axis=-1, keepdims=True) + eps)
    return (values * scale_inv * norm_gain).astype(jnp.bfloat16)


def spread_rank_rows(select_mask, factors):
    widened_rows = select_mask[:, :, None] * factors[:, None, :]
    return widened_rows.reshape(factors.shape[0], select_mask.shape[1] * factors.shape[1])


def weight_blocks(shard):
    same, other = send(shard, SAME_ROLE), send(shard, OTHER_ROLE)
    same_low, other_high = send(same, X_UP), send(other, X_DOWN)
    other_low, same_high = send(other, X_UP), send(same, X_DOWN)
    same_far, other_far = send(same_low, X_UP), send(other_high, X_DOWN)
    return [same, same_low, same_high, same_far, other, other_low, other_high, other_far]


def local(
    hidden_states,
    norm_gain,
    gate_base,
    up_base,
    down_base,
    shrink_gu,
    expand_gu,
    down_shrink_maps,
    down_expand_maps,
    token_adapter,
    adapter_slot,
):
    xi, ci, yi, hi, li = (lax.axis_index(name) for name in ALL)
    own_count, width = hidden_states.shape
    slab = gate_base.shape[0]
    units = gate_base.shape[1]
    adapter_list = adapter_slot.shape[0]
    owner_partial = adapter_list // 16
    rank = down_expand_maps.shape[0] // owner_partial
    cap = own_count // 8
    blocks = 16
    total = blocks * own_count
    adapter_range = jnp.arange(adapter_list, dtype=jnp.int32)
    group_range = jnp.arange(16, dtype=jnp.int32)

    slab_at = [((xi + dx) % 4) * 2 + (ci if half == 0 else 1 - ci) for half in range(2) for dx in X_ORDER]

    def to_own_order(array):
        return jnp.concatenate(
            [lax.dynamic_slice_in_dim(array, at * slab, slab, axis=1) for at in slab_at], axis=1
        )

    gate_up = weight_blocks(jnp.concatenate([gate_base, up_base], axis=1))
    normed = to_own_order(rms_normed(hidden_states, norm_gain))
    mine = [normed]
    for k in range(7):
        mine.append(send(mine[SOURCE[k]], TREE[k]))
    theirs = [jnp.roll(send(block, CORE), width // 2, axis=1) for block in mine]
    rows = jnp.concatenate(mine + theirs, axis=0)

    shrink = to_own_order(send(shrink_gu, SAME_ROLE))
    expand = send(expand_gu, SAME_ROLE)
    down = weight_blocks(down_base)
    down_shrink = send(down_shrink_maps, SAME_ROLE)
    down_expand = to_own_order(send(down_expand_maps, SAME_ROLE))

    matches = (token_adapter[:, None] == adapter_range[None, :]).astype(jnp.int32)
    row_slots = jnp.sum(matches * adapter_slot[None, :], axis=1).reshape(16, own_count)

    def pick(table, k):
        return jnp.where(ci == 0, table[0][k], table[1][k])

    block_y = [(yi + pick(BLOCK_Y, k)) % 4 for k in range(8)]
    block_l = [(li + pick(BLOCK_L, k)) % 2 for k in range(8)]
    block_col = jnp.stack([block_y[k] * 4 + hi * 2 + block_l[k] for k in range(8)])
    block_at = jnp.stack([(ci * 4 + block_y[k]) * 2 + block_l[k] for k in range(8)])
    chosen = (block_col[:, None] == group_range[None, :]).astype(jnp.int32)
    my_slots = jnp.sum(chosen[:, :, None] * row_slots[None], axis=1)
    my_block = jnp.concatenate([my_slots, jnp.broadcast_to(block_at[:, None], my_slots.shape)], axis=0)
    their_block = send(my_block, CORE)
    slots = jnp.concatenate([my_slots, their_block[:8]], axis=0)
    block_at = jnp.concatenate([block_at, their_block[8:, 0]], axis=0)
    to_group = (group_range[:, None] == block_at[None, :]).astype(jnp.float32)

    owners = slots // owner_partial
    owner_z = owners % 4
    owner_c = (owner_z // 2 != hi).astype(jnp.int32)
    owner_l = jnp.where(owner_c == 0, owner_z, 3 - owner_z) % 2
    owner_at = (owner_c * 4 + owners // 4) * 2 + owner_l
    owned = (owner_at[:, :, None] == group_range[None, None, :]).astype(jnp.int32)
    earlier = jnp.cumsum(owned, axis=1) - owned
    position = jnp.sum(earlier * owned, axis=2)
    target = owner_at * cap + position
    dispatch = (target[:, :, None] == jnp.arange(16 * cap, dtype=jnp.int32)).astype(jnp.bfloat16)
    group_at = (ci * 4 + yi) * 2 + li
    mine_at = group_at * cap + jnp.arange(cap, dtype=jnp.int32)
    dispatch_mine = (target[:, :, None] == mine_at).astype(jnp.bfloat16)
    role_col = yi * 4 + jnp.where(ci == 0, hi * 2 + li, 3 - hi * 2 - li)
    local_slot = slots.reshape(total) - role_col * owner_partial
    select_owned = local_slot[:, None] == jnp.arange(owner_partial, dtype=jnp.int32)[None, :]
    row_selector = (slots.reshape(total)[:, None] == adapter_range[None, :]).astype(jnp.bfloat16)

    projected = contract_trailing(rows, shrink).reshape(total, owner_partial, 2 * rank)
    rank_values = jnp.sum(projected * select_owned.astype(jnp.float32)[:, :, None], axis=1)
    rank_values = rank_values.astype(jnp.bfloat16).reshape(blocks, own_count, 2 * rank)
    packed = jnp.einsum("btp,btr->bpr", dispatch_mine, rank_values, preferred_element_type=jnp.float32)
    packed = dot(to_group, packed.reshape(blocks, cap * 2 * rank)).astype(jnp.bfloat16)
    packed = packed.reshape(1, -1, 128)
    spread = jnp.broadcast_to(packed, (16, packed.shape[1], 128))
    returned = lax.all_to_all(spread, GROUP, split_axis=0, concat_axis=0, tiled=True)
    returned = returned.reshape(16, blocks, cap * 2 * rank)
    returned = jnp.einsum(
        "ogw,gb->bow", returned, to_group.astype(jnp.bfloat16), preferred_element_type=jnp.float32
    ).astype(jnp.bfloat16)
    returned = returned.reshape(blocks, 16 * cap, 2 * rank)
    rank_rows = jnp.einsum("btp,bpr->btr", dispatch, returned, preferred_element_type=jnp.float32)
    rank_rows = rank_rows.astype(jnp.bfloat16).reshape(total, 2 * rank)

    both = dot(rows, jnp.concatenate(gate_up, axis=0))
    gate_sum = both[:, :units] + dot(spread_rank_rows(row_selector, rank_rows[:, :rank]), expand[0])
    up_sum = both[:, units:] + dot(spread_rank_rows(row_selector, rank_rows[:, rank:]), expand[1])
    hidden_rows = (jax.nn.silu(gate_sum) * up_sum).astype(jnp.bfloat16)

    down_projector = contract_trailing(hidden_rows, down_shrink).reshape(total, adapter_list, rank)
    down_part = jnp.sum(down_projector * row_selector.astype(jnp.float32)[:, :, None], axis=1)
    down_part = down_part.astype(jnp.bfloat16).reshape(blocks, own_count, rank)
    packed_down = jnp.einsum("btp,btr->bpr", dispatch, down_part, preferred_element_type=jnp.float32)
    packed_down = dot(to_group, packed_down.reshape(blocks, 16 * cap * rank)).astype(jnp.bfloat16)
    packed_down = packed_down.reshape(blocks, 16, cap * rank).transpose(1, 0, 2).reshape(16, -1, 128)
    arrived = lax.all_to_all(packed_down, GROUP, split_axis=0, concat_axis=0, tiled=True)
    down_ranks = jnp.sum(arrived.astype(jnp.float32), axis=0).astype(jnp.bfloat16)
    down_ranks = dot(to_group.T.astype(jnp.bfloat16), down_ranks.reshape(blocks, cap * rank))
    down_ranks = down_ranks.astype(jnp.bfloat16).reshape(blocks, cap, rank)
    down_ranks = jnp.einsum("btp,bpr->btr", dispatch_mine, down_ranks, preferred_element_type=jnp.float32)
    down_ranks = down_ranks.astype(jnp.bfloat16).reshape(total, rank)
    widened = spread_rank_rows(select_owned.astype(jnp.bfloat16), down_ranks)

    down_sum = dot(hidden_rows, jnp.concatenate(down, axis=1)) + dot(widened, down_expand)
    partial = down_sum.astype(jnp.bfloat16).reshape(blocks, own_count, width)

    def add(left, right):
        return (left.astype(jnp.float32) + right.astype(jnp.float32)).astype(jnp.bfloat16)

    sums = [None] * 8
    for k in (7, 6, 5, 4, 3, 2, 1, 0):
        sums[k] = add(partial[k], jnp.roll(send(partial[8 + k], CORE), width // 2, axis=1))
    for k in (6, 5, 4, 3, 2, 1, 0):
        sums[SOURCE[k]] = add(sums[SOURCE[k]], send(sums[k + 1], TREE_BACK[k]))
    result = sums[0]
    for place, at in enumerate(slab_at):
        piece = sums[0][:, place * slab : (place + 1) * slab]
        result = lax.dynamic_update_slice_in_dim(result, piece, at * slab, axis=1)
    return result


def solution(mesh):
    fine = Mesh(mesh.devices.reshape(4, 2, 4, 2, 2), ALL)
    row, col = ("x", "c"), ("y", "h", "l")
    in_specs = (
        P(row + col, None),
        P(),
        P(row, col),
        P(row, col),
        P(col, row),
        P(col, None),
        P(None, None, col),
        P(None, col),
        P(col, None),
        P(row),
        P(),
    )
    out_specs = P(row + col, None)
    return jax.shard_map(local, mesh=fine, in_specs=in_specs, out_specs=out_specs, check_vma=False)
```

```python
import jax
import jax.numpy as jnp
from jax import lax
from jax.experimental import pallas as pl
from jax.experimental.pallas import tpu as pltpu
from jax.sharding import Mesh, PartitionSpec as P


eps = 1e-05
ALL = ("x", "c", "y", "h", "l")
GROUP = ("c", "y", "l")

SOURCE = (0, 0, 0, 1, 1, 2, 4)
STEPS = (
    (("y", -1), ("y", 1), ("l", 1), ("y", -1), ("l", 1), ("l", 1), ("l", 1)),
    (("l", 1), ("y", 1), ("y", -1), ("y", 1), ("y", -1), ("y", 1), ("y", 1)),
)
BLOCK_Y = ((0, 1, -1, 0, 2, 1, -1, 2), (0, 0, -1, 1, -1, 1, 2, 2))
BLOCK_L = ((0, 0, 0, 1, 0, 1, 1, 1), (0, 1, 0, 0, 1, 1, 0, 1))
X_ORDER = (0, -1, 1, 2)


def flat(x, c, y, z):
    return (((x % 4) * 2 + c % 2) * 4 + y % 4) * 4 + z % 4


def pairs_of(move):
    return [
        (flat(x, c, y, z), flat(*move(x, c, y, z)))
        for x in range(4)
        for c in range(2)
        for y in range(4)
        for z in range(4)
    ]


def tree_pairs(k):
    def move(x, c, y, z):
        axis, shift = STEPS[c][k]
        return (x, c, y + shift, z) if axis == "y" else (x, c, y, z ^ 1)

    return pairs_of(move)


TREE = [tree_pairs(k) for k in range(7)]
TREE_BACK = [[(b, a) for a, b in pairs] for pairs in TREE]
CORE = pairs_of(lambda x, c, y, z: (x, 1 - c, y, z))
SAME_ROLE = [pair for pair in pairs_of(lambda x, c, y, z: (x, c, y, 3 - z)) if pair[0] // 16 % 2 == 1]
OTHER_ROLE = pairs_of(lambda x, c, y, z: (x, 1 - c, y, 3 - z if c == 0 else z))
X_UP = pairs_of(lambda x, c, y, z: (x + 1, c, y, z))
X_DOWN = pairs_of(lambda x, c, y, z: (x - 1, c, y, z))


HALVES = ((4, 5, 6, 7), (0, 1, 2, 3))
TILE = 512


def send(value, pairs):
    return lax.ppermute(value, ALL, pairs)


def contract_trailing(left, right):
    return lax.dot_general(
        left, right, (((left.ndim - 1,), (1,)), ((), ())), preferred_element_type=jnp.float32
    )


def dot(left, right):
    return jnp.dot(left, right, preferred_element_type=jnp.float32)


def rms_normed(states, norm_gain):
    values = states.astype(jnp.float32)
    scale_inv = lax.rsqrt(jnp.mean(values * values, axis=-1, keepdims=True) + eps)
    return (values * scale_inv * norm_gain).astype(jnp.bfloat16)


def lanes(rows, count, group):
    return lax.broadcasted_iota(jnp.int32, (rows, count), 1) // group


def kept(mask, values):
    return jnp.where(mask, values, 0.0).astype(jnp.bfloat16)


def rank_kernel(shrink, ints, ints_t, fold, *refs):
    shards, (out, rows, sems) = refs[:8], refs[8:]
    for i, shard in enumerate(shards):
        pltpu.make_async_copy(shard, rows.at[pl.ds(i * 128, 128)], sems.at[i // 4]).start()
    packed = jnp.zeros(out.shape, jnp.float32)
    for t in range(2):
        part = pl.ds(t * TILE, TILE)
        pltpu.make_async_copy(rows.at[part], rows.at[part], sems.at[t]).wait()
        group = lanes(TILE, 128, 32)
        values = kept(group == ints[part, 5:6], contract_trailing(rows[part, :], shrink[...]))
        values = kept(group == ints[part, 2:3], dot(values, fold[...]))
        place = lax.broadcasted_iota(jnp.int32, (64, TILE), 0) == ints_t[6:7, part]
        packed += dot(place.astype(jnp.bfloat16), values)
    out[...] = packed


def hidden_kernel(slab_at, ranks, ints, ints_t, expand, down_shrink, to_gate, to_up, fold, *refs):
    shards, pieces, (hidden, packed, rows, weight, total, row_sems, sem) = refs[:16], refs[16:24], refs[24:]
    slab = pieces[0].shape[0]
    for i, piece in enumerate(pieces):
        start = pl.multiple_of(slab_at[i] * slab, 128)
        pltpu.make_async_copy(piece, weight.at[pl.ds(start, slab)], sem.at[0]).start()
    for i, shard in enumerate(shards):
        pltpu.make_async_copy(shard, rows.at[pl.ds(i * 128, 128)], row_sems.at[i // 4]).start()
    total[...] = jnp.zeros(total.shape, jnp.float32)
    pltpu.make_async_copy(weight, weight, sem.at[0]).wait()
    units = hidden.shape[1]

    def tile(i, carry):
        part = pl.ds(pl.multiple_of(i * TILE, TILE), TILE)
        pltpu.make_async_copy(rows.at[part], rows.at[part], row_sems.at[i]).wait()
        both = dot(rows[part, :], weight[...])
        place = lanes(TILE, ranks.shape[0], 1) == ints[part, 1:2]
        own = kept(lanes(TILE, 128, 32) == ints[part, 2:3], dot(place.astype(jnp.bfloat16), ranks[...]))
        chosen = lanes(TILE, to_gate.shape[1], 16) == ints[part, 0:1]
        gate = both[:, :units] + dot(kept(chosen, dot(own, to_gate[...])), expand[0])
        up = both[:, units:] + dot(kept(chosen, dot(own, to_up[...])), expand[1])
        values = (gate / (1.0 + jnp.exp(-gate)) * up).astype(jnp.bfloat16)
        hidden[part, :] = values
        parts = dot(kept(chosen, contract_trailing(values, down_shrink[...])), fold[...])
        parts = kept(lanes(TILE, 128, 16) == ints[part, 4:5], parts)
        place = lax.broadcasted_iota(jnp.int32, (total.shape[0], TILE), 0) == ints_t[3:4, part]
        total[...] += dot(place.astype(jnp.bfloat16), parts)
        return carry

    lax.fori_loop(0, rows.shape[0] // TILE, tile, 0)
    packed[...] = total[...].astype(jnp.bfloat16)


def down_kernel(slab_at, hidden, ranks, ints, down_expand, widen, *refs):
    pieces, (mine, theirs, weight, sem) = refs[:8], refs[8:]
    slab = pieces[0].shape[1]
    for i, piece in enumerate(pieces):
        start = pl.multiple_of(slab_at[i] * slab, 128)
        pltpu.make_async_copy(piece, weight.at[:, pl.ds(start, slab)], sem.at[0]).start()
    pltpu.make_async_copy(weight, weight, sem.at[0]).wait()
    for t, out in enumerate((mine, theirs)):
        part = pl.ds(t * TILE, TILE)
        place = lanes(TILE, ranks.shape[0], 1) == ints[part, 7:8]
        own = kept(lanes(TILE, 128, 16) == ints[part, 4:5], dot(place.astype(jnp.bfloat16), ranks[...]))
        own = kept(lanes(TILE, 64, 16) == ints[part, 5:6], dot(own, widen[...]))
        out[...] = (dot(hidden[part, :], weight[...]) + dot(own, down_expand[...])).astype(jnp.bfloat16)


def weight_blocks(shard, ci):
    other = send(shard, OTHER_ROLE)
    same = jnp.where(ci == 0, shard, send(shard, SAME_ROLE))
    same_low, other_high = send(same, X_UP), send(other, X_DOWN)
    other_low, same_high = send(other, X_UP), send(same, X_DOWN)
    same_far, other_far = send(same_low, X_UP), send(other_high, X_DOWN)
    return [same, same_low, same_high, same_far, other, other_low, other_high, other_far]


def local(
    hidden_states,
    norm_gain,
    gate_base,
    up_base,
    down_base,
    shrink_gu,
    expand_gu,
    down_shrink_maps,
    down_expand_maps,
    token_adapter,
    adapter_slot,
):
    xi, ci, yi, hi, li = (lax.axis_index(name) for name in ALL)
    own_count, width = hidden_states.shape
    units = gate_base.shape[1]
    adapter_list = adapter_slot.shape[0]
    owner_partial = adapter_list // 16
    rank = down_expand_maps.shape[0] // owner_partial
    total = 16 * own_count
    adapter_range = jnp.arange(adapter_list, dtype=jnp.int32)
    group_range = jnp.arange(16, dtype=jnp.int32)

    slab_at = [((xi + dx) % 4) * 2 + (ci if half == 0 else 1 - ci) for half in range(2) for dx in X_ORDER]

    slab_at = jnp.stack(slab_at).astype(jnp.int32)

    gate_up = weight_blocks(jnp.concatenate([gate_base, up_base], axis=1), ci)
    mine = [rms_normed(hidden_states, norm_gain)]
    for k in range(7):
        mine.append(send(mine[SOURCE[k]], TREE[k]))
    theirs = [send(block, CORE) for block in mine]
    shards = [[part[k] for part in (mine, theirs) for k in half] for half in HALVES]

    shrink = send(shrink_gu, OTHER_ROLE)
    expand = send(expand_gu, OTHER_ROLE)
    down = weight_blocks(down_base, ci)
    down_shrink = send(down_shrink_maps, OTHER_ROLE)
    down_expand = send(down_expand_maps, OTHER_ROLE)

    matches = (token_adapter[:, None] == adapter_range[None, :]).astype(jnp.int32)
    row_slots = jnp.sum(matches * adapter_slot[None, :], axis=1).reshape(16, own_count)

    def pick(table, k):
        return jnp.where(ci == 0, table[0][k], table[1][k])

    block_y = [(yi + pick(BLOCK_Y, k)) % 4 for k in range(8)]
    block_l = [(li + pick(BLOCK_L, k)) % 2 for k in range(8)]
    block_col = jnp.stack([block_y[k] * 4 + hi * 2 + block_l[k] for k in range(8)])
    block_at = jnp.stack([(ci * 4 + block_y[k]) * 2 + block_l[k] for k in range(8)])
    chosen = (block_col[:, None] == group_range[None, :]).astype(jnp.int32)
    my_slots = jnp.sum(chosen[:, :, None] * row_slots[None], axis=1)
    my_block = jnp.concatenate([my_slots, jnp.broadcast_to(block_at[:, None], my_slots.shape)], axis=0)
    their_block = send(my_block, CORE)
    order = jnp.array([k + 8 * part for half in HALVES for part in range(2) for k in half])
    slots = jnp.concatenate([my_slots, their_block[:8]], axis=0)[order]
    block_at = jnp.concatenate([block_at, their_block[8:, 0]], axis=0)[order]

    owners = slots // owner_partial
    owner_z = owners % 4
    owner_c = (owner_z // 2 != hi).astype(jnp.int32)
    owner_l = jnp.where(owner_c == 0, owner_z, 3 - owner_z) % 2
    owner_at = (owner_c * 4 + owners // 4) * 2 + owner_l
    owned = (owner_at[:, :, None] == group_range[None, None, :]).astype(jnp.int32)
    earlier = jnp.cumsum(owned, axis=1) - owned
    position = jnp.sum(earlier * owned, axis=2)
    group_at = (ci * 4 + yi) * 2 + li
    role_col = yi * 4 + jnp.where(ci == 0, hi * 2 + li, 3 - hi * 2 - li)
    is_mine = owner_at == group_at
    block_at = jnp.broadcast_to(block_at[:, None], slots.shape)
    local_slot = slots - role_col * owner_partial
    columns = [
        slots,
        owner_at * 64 + block_at * 4 + position // 4,
        position % 4,
        owner_at * 32 + block_at * 2 + position // 8,
        position % 8,
        jnp.where(is_mine, local_slot, -1),
        jnp.where(is_mine, block_at * 4 + position // 4, -1),
        jnp.where(is_mine, block_at * 2 + position // 8, -1),
    ]
    ints_t = jnp.stack([column.reshape(total) for column in columns])
    ints = ints_t.T
    half_count = total // 2
    vmem = pl.BlockSpec(memory_space=pltpu.VMEM)
    smem = pl.BlockSpec(memory_space=pltpu.SMEM)
    stay = pl.BlockSpec(memory_space=pl.ANY)

    def matching(row_count, row_period, column_count, column_period, shift=0):
        row = jnp.arange(row_count)[:, None] % row_period - shift
        return (row == jnp.arange(column_count)[None, :] % column_period).astype(jnp.bfloat16)

    packed = sum(
        pl.pallas_call(
            rank_kernel,
            out_shape=jax.ShapeDtypeStruct((64, 128), jnp.float32),
            in_specs=[vmem] * 4 + [stay] * 8,
            out_specs=vmem,
            scratch_shapes=[pltpu.VMEM((half_count, width), jnp.bfloat16), pltpu.SemaphoreType.DMA((2,))],
            name="ranks",
        )(
            shrink,
            lax.slice_in_dim(ints, i * half_count, (i + 1) * half_count),
            lax.slice_in_dim(ints_t, i * half_count, (i + 1) * half_count, axis=1),
            matching(128, 2 * rank, 128, 2 * rank),
            *shards[i],
        )
        for i in (1, 0)
    )
    spread = jnp.broadcast_to(packed.astype(jnp.bfloat16)[None], (16, 64, 128))
    ranks = lax.all_to_all(spread, GROUP, split_axis=0, concat_axis=0, tiled=True).reshape(1024, 128)

    hidden, packed_down = pl.pallas_call(
        hidden_kernel,
        out_shape=(jax.ShapeDtypeStruct((total, units), jnp.bfloat16), jax.ShapeDtypeStruct((512, 128), jnp.bfloat16)),
        in_specs=[smem] + [vmem] * 8 + [stay] * 24,
        out_specs=(vmem, vmem),
        scratch_shapes=[
            pltpu.VMEM((total, width), jnp.bfloat16),
            pltpu.VMEM((width, 2 * units), jnp.bfloat16),
            pltpu.VMEM((512, 128), jnp.float32),
            pltpu.SemaphoreType.DMA((4,)),
            pltpu.SemaphoreType.DMA((1,)),
        ],
        name="hidden",
    )(
        slab_at,
        ranks,
        ints,
        ints_t,
        expand,
        down_shrink,
        matching(128, 2 * rank, adapter_list * rank, rank),
        matching(128, 2 * rank, adapter_list * rank, rank, rank),
        matching(adapter_list * rank, rank, 128, rank),
        *shards[0],
        *shards[1],
        *gate_up,
    )

    arrived = lax.all_to_all(packed_down.reshape(16, 32, 128), GROUP, split_axis=0, concat_axis=0, tiled=True)
    down_ranks = jnp.sum(arrived.astype(jnp.float32), axis=0).astype(jnp.bfloat16)

    def down_half(i):
        return pl.pallas_call(
            down_kernel,
            grid=(1,),
            out_shape=(jax.ShapeDtypeStruct((half_count // 2, width), jnp.bfloat16),) * 2,
            in_specs=[smem, pl.BlockSpec((half_count, units), lambda g: (i, 0))] + [vmem] * 4 + [stay] * 8,
            out_specs=(vmem, vmem),
            scratch_shapes=[pltpu.VMEM((units, width), jnp.bfloat16), pltpu.SemaphoreType.DMA((1,))],
            name="down",
        )(
            slab_at,
            hidden,
            down_ranks,
            lax.slice_in_dim(ints, i * half_count, (i + 1) * half_count),
            down_expand,
            matching(128, rank, owner_partial * rank, rank),
            *down,
        )

    def add(left, right):
        return (left.astype(jnp.float32) + right.astype(jnp.float32)).astype(jnp.bfloat16)

    sums = [None] * 8
    for i in range(2):
        mine_part, theirs_part = down_half(i)
        swapped = send(theirs_part, CORE)
        for j, k in enumerate(HALVES[i]):
            rows = slice(j * own_count, (j + 1) * own_count)
            sums[k] = add(mine_part[rows], swapped[rows])
    for k in (6, 5, 4, 3, 2, 1, 0):
        sums[SOURCE[k]] = add(sums[SOURCE[k]], send(sums[k + 1], TREE_BACK[k]))
    return sums[0]


def solution(mesh):
    fine = Mesh(mesh.devices.reshape(4, 2, 4, 2, 2), ALL)
    row, col = ("x", "c"), ("y", "h", "l")
    in_specs = (
        P(row + col, None),
        P(),
        P(row, col),
        P(row, col),
        P(col, row),
        P(col, None),
        P(None, None, col),
        P(None, col),
        P(col, None),
        P(row),
        P(),
    )
    out_specs = P(row + col, None)
    return jax.shard_map(local, mesh=fine, in_specs=in_specs, out_specs=out_specs, check_vma=False)
```

```python
import functools

import jax
import jax.numpy as jnp
from jax import lax
from jax.experimental import pallas as pl
from jax.experimental.pallas import tpu as pltpu
from jax.sharding import Mesh, PartitionSpec as P


eps = 1e-05
ALL = ("x", "c", "y", "h", "l")
GROUP = ("c", "y", "l")

SOURCE = (0, 0, 0, 1, 1, 2, 4)
STEPS = (
    (("y", -1), ("y", 1), ("l", 1), ("y", -1), ("l", 1), ("l", 1), ("l", 1)),
    (("l", 1), ("y", 1), ("y", -1), ("y", 1), ("y", -1), ("y", 1), ("y", 1)),
)
BLOCK_Y = ((0, 1, -1, 0, 2, 1, -1, 2), (0, 0, -1, 1, -1, 1, 2, 2))
BLOCK_L = ((0, 0, 0, 1, 0, 1, 1, 1), (0, 1, 0, 0, 1, 1, 0, 1))
X_ORDER = (0, -1, 1, 2)


def flat(x, c, y, z):
    return (((x % 4) * 2 + c % 2) * 4 + y % 4) * 4 + z % 4


def pairs_of(move):
    return [
        (flat(x, c, y, z), flat(*move(x, c, y, z)))
        for x in range(4)
        for c in range(2)
        for y in range(4)
        for z in range(4)
    ]


def tree_pairs(k):
    def move(x, c, y, z):
        axis, shift = STEPS[c][k]
        return (x, c, y + shift, z) if axis == "y" else (x, c, y, z ^ 1)

    return pairs_of(move)


TREE = [tree_pairs(k) for k in range(7)]
TREE_BACK = [[(b, a) for a, b in pairs] for pairs in TREE]
CORE = pairs_of(lambda x, c, y, z: (x, 1 - c, y, z))
SAME_ROLE = [pair for pair in pairs_of(lambda x, c, y, z: (x, c, y, 3 - z)) if pair[0] // 16 % 2 == 1]
OTHER_ROLE = pairs_of(lambda x, c, y, z: (x, 1 - c, y, 3 - z if c == 0 else z))
X_UP = pairs_of(lambda x, c, y, z: (x + 1, c, y, z))
X_DOWN = pairs_of(lambda x, c, y, z: (x - 1, c, y, z))


HALVES = ((7, 6, 5, 4), (0, 1, 2, 3))
ROW_BLOCKS = tuple(
    half[2 * pair + j] + 8 * part for half in HALVES for pair in range(2) for part in range(2) for j in range(2)
)
LATE_BLOCKS = 4
TILE = 256


def send(value, pairs):
    return lax.ppermute(value, ALL, pairs)


def contract_trailing(left, right):
    return lax.dot_general(
        left, right, (((left.ndim - 1,), (1,)), ((), ())), preferred_element_type=jnp.float32
    )


def dot(left, right):
    return jnp.dot(left, right, preferred_element_type=jnp.float32)


def rms_normed(states, norm_gain):
    values = states.astype(jnp.float32)
    scale_inv = lax.rsqrt(jnp.mean(values * values, axis=-1, keepdims=True) + eps)
    return (values * scale_inv * norm_gain).astype(jnp.bfloat16)


def lanes(rows, count, group):
    return lax.broadcasted_iota(jnp.int32, (rows, count), 1) // group


def kept(mask, values):
    return jnp.where(mask, values, 0.0).astype(jnp.bfloat16)


def place_kernel(at, slot_of, own, other, out, slots):
    ci, yi, hi, li = (at[i] for i in range(4))
    for part, adapters in enumerate((own, other)):
        ids = adapters[...]
        found = jnp.zeros(ids.shape, jnp.int32)
        for adapter in range(slot_of.shape[0]):
            found = jnp.where(ids == adapter, slot_of[adapter], found)
        slots[part] = found
    role_col = yi * 4 + jnp.where(ci == 0, hi * 2 + li, 3 - hi * 2 - li)
    group_at = (ci * 4 + yi) * 2 + li
    earlier = lax.broadcasted_iota(jnp.int32, (128, 128), 0) < lax.broadcasted_iota(jnp.int32, (128, 128), 1)
    for i, k in enumerate(ROW_BLOCKS):
        part, k = k // 8, k % 8
        c = ci if part == 0 else 1 - ci
        y = (yi + 4 + jnp.where(c == 0, BLOCK_Y[0][k], BLOCK_Y[1][k])) & 3
        l = (li + jnp.where(c == 0, BLOCK_L[0][k], BLOCK_L[1][k])) & 1
        block_at = (c * 4 + y) * 2 + l
        slot = slots[part, pl.ds(y * 4 + hi * 2 + l, 1), :]
        owner = slot >> 2
        owner_z = owner & 3
        native = (owner_z >> 1) == hi
        owner_l = jnp.where(native, owner_z, 3 - owner_z) & 1
        owner_at = (jnp.where(native, 0, 4) + (owner >> 2)) * 2 + owner_l
        along = jnp.broadcast_to(owner_at, (128, 128))
        alike = jnp.where((along == along.T) & earlier, 1, 0)
        position = jnp.sum(alike, axis=0, keepdims=True)
        is_mine = owner_at == group_at
        columns = (
            slot,
            owner_at * 64 + block_at * 4 + (position >> 2),
            position & 3,
            owner_at * 32 + block_at * 2 + (position >> 3),
            position & 7,
            jnp.where(is_mine, slot - role_col * 4, -1),
            jnp.where(is_mine, block_at * 4 + (position >> 2), -1),
            jnp.where(is_mine, block_at * 2 + (position >> 3), -1),
        )
        for j, column in enumerate(columns):
            out[i, j : j + 1, :] = column


def places(ints, i, first=0):
    across = jnp.concatenate([ints[first + 2 * i], ints[first + 2 * i + 1]], axis=1)
    return across.T, across


def rank_kernel(first, shrink, ints, fold, *refs):
    shards, (out, rows, sems) = refs[:-3], refs[-3:]
    for i, shard in enumerate(shards):
        pltpu.make_async_copy(shard, rows.at[pl.ds(i * 128, 128)], sems.at[i * 128 // TILE]).start()
    out[...] = jnp.zeros(out.shape, jnp.float32)

    def tile(i, carry):
        part = pl.ds(pl.multiple_of(i * TILE, TILE), TILE)
        down, across = places(ints, i, first)
        pltpu.make_async_copy(rows.at[part], rows.at[part], sems.at[i]).wait()
        group = lanes(TILE, 128, 32)
        values = kept(group == down[:, 5:6], contract_trailing(rows[part, :], shrink[...]))
        values = kept(group == down[:, 2:3], dot(values, fold[...]))
        place = lax.broadcasted_iota(jnp.int32, (64, TILE), 0) == across[6:7]
        out[...] += dot(place.astype(jnp.bfloat16), values)
        return carry

    lax.fori_loop(0, rows.shape[0] // TILE, tile, 0)


def hidden_kernel(slab_at, ranks, ints, expand, down_shrink, to_gate, to_up, fold, *refs):
    shards, pieces, (hidden, packed, rows, weight, total, row_sems, sem) = refs[:16], refs[16:24], refs[24:]
    slab = pieces[0].shape[0]
    for i, piece in enumerate(pieces):
        start = pl.multiple_of(slab_at[i] * slab, 128)
        pltpu.make_async_copy(piece, weight.at[pl.ds(start, slab)], sem.at[0]).start()
    for i, shard in enumerate(shards):
        pltpu.make_async_copy(shard, rows.at[pl.ds(i * 128, 128)], row_sems.at[i * 128 // TILE]).start()
    total[...] = jnp.zeros(total.shape, jnp.float32)
    pltpu.make_async_copy(weight, weight, sem.at[0]).wait()
    units = hidden.shape[1]

    def tile(i, carry):
        part = pl.ds(pl.multiple_of(i * TILE, TILE), TILE)
        down, across = places(ints, i)
        pltpu.make_async_copy(rows.at[part], rows.at[part], row_sems.at[i]).wait()
        both = dot(rows[part, :], weight[...])
        place = lanes(TILE, ranks.shape[0], 1) == down[:, 1:2]
        own = kept(lanes(TILE, 128, 32) == down[:, 2:3], dot(place.astype(jnp.bfloat16), ranks[...]))
        chosen = lanes(TILE, to_gate.shape[1], 16) == down[:, 0:1]
        gate = both[:, :units] + dot(kept(chosen, dot(own, to_gate[...])), expand[0])
        up = both[:, units:] + dot(kept(chosen, dot(own, to_up[...])), expand[1])
        values = (gate / (1.0 + jnp.exp(-gate)) * up).astype(jnp.bfloat16)
        hidden[part, :] = values
        parts = dot(kept(chosen, contract_trailing(values, down_shrink[...])), fold[...])
        parts = kept(lanes(TILE, 128, 16) == down[:, 4:5], parts)
        place = lax.broadcasted_iota(jnp.int32, (total.shape[0], TILE), 0) == across[3:4]
        total[...] += dot(place.astype(jnp.bfloat16), parts)
        return carry

    lax.fori_loop(0, rows.shape[0] // TILE, tile, 0)
    packed[...] = total[...].astype(jnp.bfloat16)


def down_kernel(first, slab_at, hidden, ranks, ints, down_expand, widen, *refs):
    pieces, (mine, theirs, weight, sem) = refs[:8], refs[8:]
    slab = pieces[0].shape[1]
    for i, piece in enumerate(pieces):
        start = pl.multiple_of(slab_at[i] * slab, 128)
        pltpu.make_async_copy(piece, weight.at[:, pl.ds(start, slab)], sem.at[0]).start()
    pltpu.make_async_copy(weight, weight, sem.at[0]).wait()
    for t, out in enumerate((mine, theirs)):

        def tile(i, carry):
            at = pl.ds(pl.multiple_of(i * TILE, TILE), TILE)
            part = pl.ds(pl.multiple_of((2 * i + t) * TILE, TILE), TILE)
            numbers, _ = places(ints, 2 * i + t, first)
            place = lanes(TILE, ranks.shape[0], 1) == numbers[:, 7:8]
            own = kept(lanes(TILE, 128, 16) == numbers[:, 4:5], dot(place.astype(jnp.bfloat16), ranks[...]))
            own = kept(lanes(TILE, 64, 16) == numbers[:, 5:6], dot(own, widen[...]))
            out[at, :] = (dot(hidden[part, :], weight[...]) + dot(own, down_expand[...])).astype(jnp.bfloat16)
            return carry

        lax.fori_loop(0, out.shape[0] // TILE, tile, 0)


def weight_blocks(shard, ci):
    other = send(shard, OTHER_ROLE)
    same = jnp.where(ci == 0, shard, send(shard, SAME_ROLE))
    same_low, other_high = send(same, X_UP), send(other, X_DOWN)
    other_low, same_high = send(other, X_UP), send(same, X_DOWN)
    same_far, other_far = send(same_low, X_UP), send(other_high, X_DOWN)
    return [same, same_low, same_high, same_far, other, other_low, other_high, other_far]


def local(
    hidden_states,
    norm_gain,
    gate_base,
    up_base,
    down_base,
    shrink_gu,
    expand_gu,
    down_shrink_maps,
    down_expand_maps,
    token_adapter,
    adapter_slot,
):
    xi, ci, yi, hi, li = (lax.axis_index(name) for name in ALL)
    own_count, width = hidden_states.shape
    units = gate_base.shape[1]
    adapter_list = adapter_slot.shape[0]
    owner_partial = adapter_list // 16
    rank = down_expand_maps.shape[0] // owner_partial
    total = 16 * own_count
    adapter_range = jnp.arange(adapter_list, dtype=jnp.int32)
    group_range = jnp.arange(16, dtype=jnp.int32)

    slab_at = [((xi + dx) % 4) * 2 + (ci if half == 0 else 1 - ci) for half in range(2) for dx in X_ORDER]

    slab_at = jnp.stack(slab_at).astype(jnp.int32)

    gate_up = weight_blocks(jnp.concatenate([gate_base, up_base], axis=1), ci)
    mine = [rms_normed(hidden_states, norm_gain)]
    for k in range(7):
        mine.append(send(mine[SOURCE[k]], TREE[k]))
    theirs = [send(block, CORE) for block in mine]
    shards = [(mine + theirs)[k] for k in ROW_BLOCKS]

    shrink = send(shrink_gu, OTHER_ROLE)
    expand = send(expand_gu, OTHER_ROLE)
    down = weight_blocks(down_base, ci)
    down_shrink = send(down_shrink_maps, OTHER_ROLE)
    down_expand = send(down_expand_maps, OTHER_ROLE)

    half_count = total // 2
    vmem = pl.BlockSpec(memory_space=pltpu.VMEM)
    smem = pl.BlockSpec(memory_space=pltpu.SMEM)
    stay = pl.BlockSpec(memory_space=pl.ANY)

    def matching(row_count, row_period, column_count, column_period, shift=0):
        row = jnp.arange(row_count)[:, None] % row_period - shift
        return (row == jnp.arange(column_count)[None, :] % column_period).astype(jnp.bfloat16)

    own_adapters = token_adapter.reshape(16, own_count)
    ints = pl.pallas_call(
        place_kernel,
        out_shape=jax.ShapeDtypeStruct((16, 8, own_count), jnp.int32),
        in_specs=[smem, smem, vmem, vmem],
        out_specs=vmem,
        scratch_shapes=[pltpu.VMEM((2, 16, own_count), jnp.int32)],
        name="places",
    )(jnp.stack([ci, yi, hi, li]), adapter_slot, own_adapters, send(own_adapters, CORE))

    def ranks_of(first, last):
        count = (last - first) * own_count
        return pl.pallas_call(
            functools.partial(rank_kernel, first),
            out_shape=jax.ShapeDtypeStruct((64, 128), jnp.float32),
            in_specs=[vmem] * 3 + [stay] * (last - first),
            out_specs=vmem,
            scratch_shapes=[
                pltpu.VMEM((count, width), jnp.bfloat16),
                pltpu.SemaphoreType.DMA((count // TILE,)),
            ],
            name="ranks",
        )(shrink, ints, matching(128, 2 * rank, 128, 2 * rank), *shards[first:last])

    packed = ranks_of(LATE_BLOCKS, 16) + ranks_of(0, LATE_BLOCKS)
    spread = jnp.broadcast_to(packed.astype(jnp.bfloat16)[None], (16, 64, 128))
    ranks = lax.all_to_all(spread, GROUP, split_axis=0, concat_axis=0, tiled=True).reshape(1024, 128)

    hidden, packed_down = pl.pallas_call(
        hidden_kernel,
        out_shape=(jax.ShapeDtypeStruct((total, units), jnp.bfloat16), jax.ShapeDtypeStruct((512, 128), jnp.bfloat16)),
        in_specs=[smem] + [vmem] * 7 + [stay] * 24,
        out_specs=(vmem, vmem),
        scratch_shapes=[
            pltpu.VMEM((total, width), jnp.bfloat16),
            pltpu.VMEM((width, 2 * units), jnp.bfloat16),
            pltpu.VMEM((512, 128), jnp.float32),
            pltpu.SemaphoreType.DMA((total // TILE,)),
            pltpu.SemaphoreType.DMA((1,)),
        ],
        name="hidden",
    )(
        slab_at,
        ranks,
        ints,
        expand,
        down_shrink,
        matching(128, 2 * rank, adapter_list * rank, rank),
        matching(128, 2 * rank, adapter_list * rank, rank, rank),
        matching(adapter_list * rank, rank, 128, rank),
        *shards,
        *gate_up,
    )

    arrived = lax.all_to_all(
        packed_down.reshape(16, 32, 128), GROUP, split_axis=0, concat_axis=0, tiled=True
    )
    down_ranks = jnp.sum(arrived.astype(jnp.float32), axis=0).astype(jnp.bfloat16)

    def down_half(i):
        return pl.pallas_call(
            functools.partial(down_kernel, 8 * i),
            grid=(1,),
            out_shape=(jax.ShapeDtypeStruct((half_count // 2, width), jnp.bfloat16),) * 2,
            in_specs=[smem, pl.BlockSpec((half_count, units), lambda g: (i, 0))] + [vmem] * 4 + [stay] * 8,
            out_specs=(vmem, vmem),
            scratch_shapes=[pltpu.VMEM((units, width), jnp.bfloat16), pltpu.SemaphoreType.DMA((1,))],
            name="down",
        )(
            slab_at,
            hidden,
            down_ranks,
            ints,
            down_expand,
            matching(128, rank, owner_partial * rank, rank),
            *down,
        )

    def add(left, right):
        return (left.astype(jnp.float32) + right.astype(jnp.float32)).astype(jnp.bfloat16)

    sums = [None] * 8
    for i in range(2):
        mine_part, theirs_part = down_half(i)
        swapped = send(theirs_part, CORE)
        added = [
            add(mine_part[j * own_count : (j + 1) * own_count], swapped[j * own_count : (j + 1) * own_count])
            for j in range(4)
        ]
        for k, value in zip(HALVES[i], lax.optimization_barrier(added)):
            sums[k] = value
    for k in (6, 5, 4, 3, 2, 1, 0):
        sums[SOURCE[k]] = add(sums[SOURCE[k]], send(sums[k + 1], TREE_BACK[k]))
    return sums[0]


def solution(mesh):
    fine = Mesh(mesh.devices.reshape(4, 2, 4, 2, 2), ALL)
    row, col = ("x", "c"), ("y", "h", "l")
    in_specs = (
        P(row + col, None),
        P(),
        P(row, col),
        P(row, col),
        P(col, row),
        P(col, None),
        P(None, None, col),
        P(None, col),
        P(col, None),
        P(row),
        P(),
    )
    out_specs = P(row + col, None)
    return jax.shard_map(local, mesh=fine, in_specs=in_specs, out_specs=out_specs, check_vma=False)
```

```python
import functools

import jax
import jax.numpy as jnp
from jax import lax
from jax.experimental import pallas as pl
from jax.experimental.pallas import tpu as pltpu
from jax.sharding import Mesh, PartitionSpec as P


eps = 1e-05
ALL = ("x", "c", "y", "h", "l")
GROUP = ("c", "y", "l")

SOURCE = (0, 0, 0, 1, 1, 2, 4)
STEPS = (
    (("y", -1), ("y", 1), ("l", 1), ("y", -1), ("l", 1), ("l", 1), ("l", 1)),
    (("l", 1), ("y", 1), ("y", -1), ("y", 1), ("y", -1), ("y", 1), ("y", 1)),
)
BLOCK_Y = ((0, 1, -1, 0, 2, 1, -1, 2), (0, 0, -1, 1, -1, 1, 2, 2))
BLOCK_L = ((0, 0, 0, 1, 0, 1, 1, 1), (0, 1, 0, 0, 1, 1, 0, 1))
X_ORDER = (0, -1, 1, 2)


def flat(x, c, y, z):
    return (((x % 4) * 2 + c % 2) * 4 + y % 4) * 4 + z % 4


def pairs_of(move):
    return [
        (flat(x, c, y, z), flat(*move(x, c, y, z)))
        for x in range(4)
        for c in range(2)
        for y in range(4)
        for z in range(4)
    ]


def tree_pairs(k):
    def move(x, c, y, z):
        axis, shift = STEPS[c][k]
        return (x, c, y + shift, z) if axis == "y" else (x, c, y, z ^ 1)

    return pairs_of(move)


TREE = [tree_pairs(k) for k in range(7)]
TREE_BACK = [[(b, a) for a, b in pairs] for pairs in TREE]
CORE = pairs_of(lambda x, c, y, z: (x, 1 - c, y, z))
SAME_ROLE = [pair for pair in pairs_of(lambda x, c, y, z: (x, c, y, 3 - z)) if pair[0] // 16 % 2 == 1]
OTHER_ROLE = pairs_of(lambda x, c, y, z: (x, 1 - c, y, 3 - z if c == 0 else z))
X_UP = pairs_of(lambda x, c, y, z: (x + 1, c, y, z))
X_DOWN = pairs_of(lambda x, c, y, z: (x - 1, c, y, z))


HALVES = ((7, 6, 5, 4), (3, 2, 1, 0))
ROW_BLOCKS = tuple(
    half[2 * pair + j] + 8 * part for half in HALVES for pair in range(2) for part in range(2) for j in range(2)
)
LATE_BLOCKS = 4
TILE = 256


def send(value, pairs):
    return lax.ppermute(value, ALL, pairs)


def contract_trailing(left, right):
    return lax.dot_general(
        left, right, (((left.ndim - 1,), (1,)), ((), ())), preferred_element_type=jnp.float32
    )


def dot(left, right):
    return jnp.dot(left, right, preferred_element_type=jnp.float32)


def rms_normed(states, norm_gain):
    values = states.astype(jnp.float32)
    scale_inv = lax.rsqrt(jnp.mean(values * values, axis=-1, keepdims=True) + eps)
    return (values * scale_inv * norm_gain).astype(jnp.bfloat16)


def lanes(rows, count, group):
    return lax.broadcasted_iota(jnp.int32, (rows, count), 1) // group


def kept(mask, values):
    return jnp.where(mask, values, 0.0).astype(jnp.bfloat16)


def place_kernel(at, slot_of, own, other, out, slots):
    ci, yi, hi, li = (at[i] for i in range(4))
    for part, adapters in enumerate((own, other)):
        ids = adapters[...]
        found = jnp.zeros(ids.shape, jnp.int32)
        for adapter in range(slot_of.shape[0]):
            found = jnp.where(ids == adapter, slot_of[adapter], found)
        slots[part] = found
    role_col = yi * 4 + jnp.where(ci == 0, hi * 2 + li, 3 - hi * 2 - li)
    group_at = (ci * 4 + yi) * 2 + li
    earlier = lax.broadcasted_iota(jnp.int32, (128, 128), 0) < lax.broadcasted_iota(jnp.int32, (128, 128), 1)
    token = lax.broadcasted_iota(jnp.int32, (1, 128), 1)
    for i, k in enumerate(ROW_BLOCKS):
        part, k = k // 8, k % 8
        c = ci if part == 0 else 1 - ci
        y = (yi + 4 + jnp.where(c == 0, BLOCK_Y[0][k], BLOCK_Y[1][k])) & 3
        l = (li + jnp.where(c == 0, BLOCK_L[0][k], BLOCK_L[1][k])) & 1
        block_at = (c * 4 + y) * 2 + l
        slot = slots[part, pl.ds(y * 4 + hi * 2 + l, 1), :]
        owner = slot >> 2
        owner_z = owner & 3
        native = (owner_z >> 1) == hi
        owner_l = jnp.where(native, owner_z, 3 - owner_z) & 1
        owner_at = (jnp.where(native, 0, 4) + (owner >> 2)) * 2 + owner_l
        along = jnp.broadcast_to(owner_at, (128, 128))
        alike = jnp.where((along == along.T) & earlier, 1, 0)
        position = jnp.sum(alike, axis=0, keepdims=True)
        is_mine = owner_at == group_at
        columns = (
            slot,
            owner_at * 64 + block_at * 4 + (position >> 2),
            position & 3,
            block_at * 16 + (token >> 3),
            token & 7,
            jnp.where(is_mine, slot - role_col * 4, -1),
            jnp.where(is_mine, block_at * 4 + (position >> 2), -1),
            token,
        )
        for j, column in enumerate(columns):
            out[i, j : j + 1, :] = column


def places(ints, i, first=0):
    across = jnp.concatenate([ints[first + 2 * i], ints[first + 2 * i + 1]], axis=1)
    return across.T, across


def rank_kernel(first, shrink, ints, fold, *refs):
    shards, (out, rows, sems) = refs[:-3], refs[-3:]
    for i, shard in enumerate(shards):
        pltpu.make_async_copy(shard, rows.at[pl.ds(i * 128, 128)], sems.at[i * 128 // TILE]).start()
    out[...] = jnp.zeros(out.shape, jnp.float32)

    def tile(i, carry):
        part = pl.ds(pl.multiple_of(i * TILE, TILE), TILE)
        down, across = places(ints, i, first)
        pltpu.make_async_copy(rows.at[part], rows.at[part], sems.at[i]).wait()
        group = lanes(TILE, 128, 32)
        values = kept(group == down[:, 5:6], contract_trailing(rows[part, :], shrink[...]))
        values = kept(group == down[:, 2:3], dot(values, fold[...]))
        place = lax.broadcasted_iota(jnp.int32, (64, TILE), 0) == across[6:7]
        out[...] += dot(place.astype(jnp.bfloat16), values)
        return carry

    lax.fori_loop(0, rows.shape[0] // TILE, tile, 0)


def hidden_kernel(first, slab_at, ranks, ints, expand, down_shrink, to_gate, to_up, fold, *refs):
    shards, pieces, (hidden, packed, rows, weight, row_sems, sem) = refs[:8], refs[8:16], refs[16:]
    slab = pieces[0].shape[0]
    for i, piece in enumerate(pieces):
        start = pl.multiple_of(slab_at[i] * slab, 128)
        pltpu.make_async_copy(piece, weight.at[pl.ds(start, slab)], sem.at[0]).start()
    for i, shard in enumerate(shards):
        pltpu.make_async_copy(shard, rows.at[pl.ds(i * 128, 128)], row_sems.at[i * 128 // TILE]).start()
    packed[...] = jnp.zeros(packed.shape, jnp.float32)
    pltpu.make_async_copy(weight, weight, sem.at[0]).wait()
    units = hidden.shape[1]

    def tile(i, carry):
        part = pl.ds(pl.multiple_of(i * TILE, TILE), TILE)
        down, across = places(ints, i, first)
        pltpu.make_async_copy(rows.at[part], rows.at[part], row_sems.at[i]).wait()
        both = dot(rows[part, :], weight[...])
        place = lanes(TILE, ranks.shape[0], 1) == down[:, 1:2]
        own = kept(lanes(TILE, 128, 32) == down[:, 2:3], dot(place.astype(jnp.bfloat16), ranks[...]))
        chosen = lanes(TILE, to_gate.shape[1], 16) == down[:, 0:1]
        gate = both[:, :units] + dot(kept(chosen, dot(own, to_gate[...])), expand[0])
        up = both[:, units:] + dot(kept(chosen, dot(own, to_up[...])), expand[1])
        values = (gate / (1.0 + jnp.exp(-gate)) * up).astype(jnp.bfloat16)
        hidden[part, :] = values
        parts = dot(kept(chosen, contract_trailing(values, down_shrink[...])), fold[...])
        parts = kept(lanes(TILE, 128, 16) == down[:, 4:5], parts)
        place = lax.broadcasted_iota(jnp.int32, (packed.shape[0], TILE), 0) == across[3:4]
        packed[...] += dot(place.astype(jnp.bfloat16), parts)
        return carry

    lax.fori_loop(0, rows.shape[0] // TILE, tile, 0)


def down_kernel(slab_at, hidden, *refs):
    pieces, (mine, theirs, weight, sem) = refs[:8], refs[8:]
    slab = pieces[0].shape[1]
    for i, piece in enumerate(pieces):
        start = pl.multiple_of(slab_at[i] * slab, 128)
        pltpu.make_async_copy(piece, weight.at[:, pl.ds(start, slab)], sem.at[0]).start()
    pltpu.make_async_copy(weight, weight, sem.at[0]).wait()
    columns = weight.shape[1] // 4

    def chunk(i, carry):
        part = pl.ds(pl.multiple_of(i * columns, 128), columns)
        both = dot(hidden[...], weight[:, part]).astype(jnp.bfloat16)
        mine[:, part] = both[:TILE]
        theirs[:, part] = both[TILE:]
        return carry

    lax.fori_loop(0, 4, chunk, 0)


def adapter_kernel(ranks, ints, lane_slot, spread, *refs):
    maps, (mine, theirs, whole, sem) = refs[:8], refs[8:]
    for i, piece in enumerate(maps):
        pltpu.make_async_copy(piece, whole.at[pl.ds(i * 64, 64)], sem.at[0]).start()
    pltpu.make_async_copy(whole, whole, sem.at[0]).wait()
    for t, out in enumerate((mine, theirs)):
        down = ints[ROW_BLOCKS.index(8 * t)].T
        place = lanes(128, 16, 1) == down[:, 7:8] >> 3
        own = kept(lanes(128, 128, 16) == down[:, 4:5], dot(place.astype(jnp.bfloat16), ranks[t]))
        own = kept(lane_slot[...] == down[:, 0:1], dot(own, spread[...]))
        out[...] = dot(own, whole[...]).astype(jnp.bfloat16)


def weight_blocks(shard, ci):
    other = send(shard, OTHER_ROLE)
    same = jnp.where(ci == 0, shard, send(shard, SAME_ROLE))
    same_low, other_high = send(same, X_UP), send(other, X_DOWN)
    other_low, same_high = send(other, X_UP), send(same, X_DOWN)
    same_far, other_far = send(same_low, X_UP), send(other_high, X_DOWN)
    return [same, same_low, same_high, same_far, other, other_low, other_high, other_far]


def local(
    hidden_states,
    norm_gain,
    gate_base,
    up_base,
    down_base,
    shrink_gu,
    expand_gu,
    down_shrink_maps,
    down_expand_maps,
    token_adapter,
    adapter_slot,
):
    xi, ci, yi, hi, li = (lax.axis_index(name) for name in ALL)
    own_count, width = hidden_states.shape
    units = gate_base.shape[1]
    adapter_list = adapter_slot.shape[0]
    owner_partial = adapter_list // 16
    rank = down_expand_maps.shape[0] // owner_partial
    total = 16 * own_count

    slab_at = [((xi + dx) % 4) * 2 + (ci if half == 0 else 1 - ci) for half in range(2) for dx in X_ORDER]

    slab_at = jnp.stack(slab_at).astype(jnp.int32)

    gate_up = weight_blocks(jnp.concatenate([gate_base, up_base], axis=1), ci)
    mine = [rms_normed(hidden_states, norm_gain)]
    for k in range(7):
        mine.append(send(mine[SOURCE[k]], TREE[k]))
    theirs = [send(block, CORE) for block in mine]
    shards = [(mine + theirs)[k] for k in ROW_BLOCKS]

    shrink = send(shrink_gu, OTHER_ROLE)
    expand = send(expand_gu, OTHER_ROLE)
    down = weight_blocks(down_base, ci)
    down_shrink = send(down_shrink_maps, OTHER_ROLE)
    down_expand = send(down_expand_maps, OTHER_ROLE)

    maps = [down_expand]
    for k in range(7):
        maps.append(send(maps[SOURCE[k]], TREE[k]))

    def pick(table, k):
        return jnp.where(ci == 0, table[0][k], table[1][k])

    map_slots = []
    for k in range(8):
        from_y, from_l = (yi + pick(BLOCK_Y, k)) % 4, (li + pick(BLOCK_L, k)) % 2
        map_slots.append((from_y * 4 + jnp.where(ci == 0, hi * 2 + from_l, 3 - hi * 2 - from_l)) * owner_partial)
    lane_slot = jnp.stack(map_slots).astype(jnp.int32)[:, None] + jnp.arange(64, dtype=jnp.int32)[None, :] // rank
    lane_slot = lane_slot.reshape(1, 512)

    half_count = total // 2
    vmem = pl.BlockSpec(memory_space=pltpu.VMEM)
    smem = pl.BlockSpec(memory_space=pltpu.SMEM)
    stay = pl.BlockSpec(memory_space=pl.ANY)

    def matching(row_count, row_period, column_count, column_period, shift=0):
        row = jnp.arange(row_count)[:, None] % row_period - shift
        return (row == jnp.arange(column_count)[None, :] % column_period).astype(jnp.bfloat16)

    own_adapters = token_adapter.reshape(16, own_count)
    ints = pl.pallas_call(
        place_kernel,
        out_shape=jax.ShapeDtypeStruct((16, 8, own_count), jnp.int32),
        in_specs=[smem, smem, vmem, vmem],
        out_specs=vmem,
        scratch_shapes=[pltpu.VMEM((2, 16, own_count), jnp.int32)],
        name="places",
    )(jnp.stack([ci, yi, hi, li]), adapter_slot, own_adapters, send(own_adapters, CORE))

    def ranks_of(first, last):
        count = (last - first) * own_count
        return pl.pallas_call(
            functools.partial(rank_kernel, first),
            out_shape=jax.ShapeDtypeStruct((64, 128), jnp.float32),
            in_specs=[vmem] * 3 + [stay] * (last - first),
            out_specs=vmem,
            scratch_shapes=[
                pltpu.VMEM((count, width), jnp.bfloat16),
                pltpu.SemaphoreType.DMA((count // TILE,)),
            ],
            name="ranks",
        )(shrink, ints, matching(128, 2 * rank, 128, 2 * rank), *shards[first:last])

    packed = ranks_of(LATE_BLOCKS, 16) + ranks_of(0, LATE_BLOCKS)
    spread = jnp.broadcast_to(packed.astype(jnp.bfloat16)[None], (16, 64, 128))
    ranks = lax.all_to_all(spread, GROUP, split_axis=0, concat_axis=0, tiled=True).reshape(1024, 128)

    def hidden_half(i):
        return pl.pallas_call(
            functools.partial(hidden_kernel, 8 * i),
            out_shape=(
                jax.ShapeDtypeStruct((half_count, units), jnp.bfloat16),
                jax.ShapeDtypeStruct((256, 128), jnp.float32),
            ),
            in_specs=[smem] + [vmem] * 7 + [stay] * 16,
            out_specs=(vmem, vmem),
            scratch_shapes=[
                pltpu.VMEM((half_count, width), jnp.bfloat16),
                pltpu.VMEM((width, 2 * units), jnp.bfloat16),
                pltpu.SemaphoreType.DMA((half_count // TILE,)),
                pltpu.SemaphoreType.DMA((1,)),
            ],
            name="hidden",
        )(
            slab_at,
            ranks,
            ints,
            expand,
            down_shrink,
            matching(128, 2 * rank, adapter_list * rank, rank),
            matching(128, 2 * rank, adapter_list * rank, rank, rank),
            matching(adapter_list * rank, rank, 128, rank),
            *shards[8 * i : 8 * i + 8],
            *gate_up,
        )

    def down_quarter(hidden, i):
        return pl.pallas_call(
            down_kernel,
            grid=(1,),
            out_shape=(jax.ShapeDtypeStruct((TILE, width), jnp.bfloat16),) * 2,
            in_specs=[smem, pl.BlockSpec((2 * TILE, units), lambda g: (i, 0))] + [stay] * 8,
            out_specs=(vmem, vmem),
            scratch_shapes=[pltpu.VMEM((units, width), jnp.bfloat16), pltpu.SemaphoreType.DMA((1,))],
            name="down",
        )(slab_at, hidden, *down)

    def add(left, right):
        return (left.astype(jnp.float32) + right.astype(jnp.float32)).astype(jnp.bfloat16)

    sums = [None] * 8
    packed_down = []
    for i in range(2):
        hidden, packed = hidden_half(i)
        packed_down.append(packed)
        for j in range(2):
            mine_part, theirs_part = down_quarter(hidden, j)
            swapped = send(theirs_part, CORE)
            added = [add(mine_part[at : at + 128], swapped[at : at + 128]) for at in (0, 128)]
            for k, value in zip(HALVES[i][2 * j : 2 * j + 2], lax.optimization_barrier(added)):
                sums[k] = value

    packed_down = (packed_down[0] + packed_down[1]).astype(jnp.bfloat16).reshape(16, 16, 128)
    arrived = lax.all_to_all(packed_down, GROUP, split_axis=0, concat_axis=0, tiled=True)
    down_ranks = jnp.sum(arrived.astype(jnp.float32), axis=0).astype(jnp.bfloat16)
    both_ranks = jnp.stack([down_ranks, send(down_ranks, CORE)])
    own_adapter, their_adapter = pl.pallas_call(
        adapter_kernel,
        out_shape=(jax.ShapeDtypeStruct((own_count, width), jnp.bfloat16),) * 2,
        in_specs=[vmem] * 4 + [stay] * 8,
        out_specs=(vmem, vmem),
        scratch_shapes=[pltpu.VMEM((512, width), jnp.bfloat16), pltpu.SemaphoreType.DMA((1,))],
        name="adapters",
    )(both_ranks, ints, lane_slot, matching(128, rank, 512, rank), *maps)
    adapter_term = own_adapter.astype(jnp.float32) + send(their_adapter, CORE).astype(jnp.float32)

    for k in (6, 5, 4, 3, 2, 1):
        sums[SOURCE[k]] = add(sums[SOURCE[k]], send(sums[k + 1], TREE_BACK[k]))
    last = send(sums[1], TREE_BACK[0]).astype(jnp.float32)
    return (sums[0].astype(jnp.float32) + last + adapter_term).astype(jnp.bfloat16)


def solution(mesh):
    fine = Mesh(mesh.devices.reshape(4, 2, 4, 2, 2), ALL)
    row, col = ("x", "c"), ("y", "h", "l")
    in_specs = (
        P(row + col, None),
        P(),
        P(row, col),
        P(row, col),
        P(col, row),
        P(col, None),
        P(None, None, col),
        P(None, col),
        P(col, None),
        P(row),
        P(),
    )
    out_specs = P(row + col, None)
    return jax.shard_map(local, mesh=fine, in_specs=in_specs, out_specs=out_specs, check_vma=False)
```

```python
import functools

import jax
import jax.numpy as jnp
from jax import lax
from jax.experimental import pallas as pl
from jax.experimental.pallas import tpu as pltpu
from jax.sharding import Mesh, PartitionSpec as P


eps = 1e-05
ALL = ("x", "c", "y", "h", "l")
GROUP = ("c", "y", "l")

SOURCE = (0, 0, 0, 1, 1, 2, 4)
STEPS = (
    (("y", -1), ("y", 1), ("l", 1), ("y", -1), ("l", 1), ("l", 1), ("l", 1)),
    (("l", 1), ("y", 1), ("y", -1), ("y", 1), ("y", -1), ("y", 1), ("y", 1)),
)
BLOCK_Y = ((0, 1, -1, 0, 2, 1, -1, 2), (0, 0, -1, 1, -1, 1, 2, 2))
BLOCK_L = ((0, 0, 0, 1, 0, 1, 1, 1), (0, 1, 0, 0, 1, 1, 0, 1))
X_ORDER = (0, -1, 1, 2)


def flat(x, c, y, z):
    return (((x % 4) * 2 + c % 2) * 4 + y % 4) * 4 + z % 4


def pairs_of(move):
    return [
        (flat(x, c, y, z), flat(*move(x, c, y, z)))
        for x in range(4)
        for c in range(2)
        for y in range(4)
        for z in range(4)
    ]


def tree_pairs(k):
    def move(x, c, y, z):
        axis, shift = STEPS[c][k]
        return (x, c, y + shift, z) if axis == "y" else (x, c, y, z ^ 1)

    return pairs_of(move)


TREE = [tree_pairs(k) for k in range(7)]
TREE_BACK = [[(b, a) for a, b in pairs] for pairs in TREE]
CORE = pairs_of(lambda x, c, y, z: (x, 1 - c, y, z))
SAME_ROLE = [pair for pair in pairs_of(lambda x, c, y, z: (x, c, y, 3 - z)) if pair[0] // 16 % 2 == 1]
OTHER_ROLE = pairs_of(lambda x, c, y, z: (x, 1 - c, y, 3 - z if c == 0 else z))
X_UP = pairs_of(lambda x, c, y, z: (x + 1, c, y, z))
X_DOWN = pairs_of(lambda x, c, y, z: (x - 1, c, y, z))


HALVES = ((7, 6, 5, 4), (3, 2, 1, 0))
ROW_BLOCKS = tuple(
    half[2 * pair + j] + 8 * part for half in HALVES for pair in range(2) for part in range(2) for j in range(2)
)
LATE_BLOCKS = 4
TILE = 256


def send(value, pairs):
    return lax.ppermute(value, ALL, pairs)


def contract_trailing(left, right):
    return lax.dot_general(
        left, right, (((left.ndim - 1,), (1,)), ((), ())), preferred_element_type=jnp.float32
    )


def dot(left, right):
    return jnp.dot(left, right, preferred_element_type=jnp.float32)


def rms_normed(states, norm_gain):
    values = states.astype(jnp.float32)
    scale_inv = lax.rsqrt(jnp.mean(values * values, axis=-1, keepdims=True) + eps)
    return (values * scale_inv * norm_gain).astype(jnp.bfloat16)


def lanes(rows, count, group):
    return lax.broadcasted_iota(jnp.int32, (rows, count), 1) // group


def kept(mask, values):
    return jnp.where(mask, values, 0.0).astype(jnp.bfloat16)


def place_kernel(at, slot_of, own, other, out, slots):
    ci, yi, hi, li = (at[i] for i in range(4))
    for part, adapters in enumerate((own, other)):
        ids = adapters[...]
        found = jnp.zeros(ids.shape, jnp.int32)
        for adapter in range(slot_of.shape[0]):
            found = jnp.where(ids == adapter, slot_of[adapter], found)
        slots[part] = found
    role_col = yi * 4 + jnp.where(ci == 0, hi * 2 + li, 3 - hi * 2 - li)
    group_at = (ci * 4 + yi) * 2 + li
    earlier = lax.broadcasted_iota(jnp.int32, (128, 128), 0) < lax.broadcasted_iota(jnp.int32, (128, 128), 1)
    token = lax.broadcasted_iota(jnp.int32, (1, 128), 1)
    for i, k in enumerate(ROW_BLOCKS):
        part, k = k // 8, k % 8
        c = ci if part == 0 else 1 - ci
        y = (yi + 4 + jnp.where(c == 0, BLOCK_Y[0][k], BLOCK_Y[1][k])) & 3
        l = (li + jnp.where(c == 0, BLOCK_L[0][k], BLOCK_L[1][k])) & 1
        block_at = (c * 4 + y) * 2 + l
        slot = slots[part, pl.ds(y * 4 + hi * 2 + l, 1), :]
        owner = slot >> 2
        owner_z = owner & 3
        native = (owner_z >> 1) == hi
        owner_l = jnp.where(native, owner_z, 3 - owner_z) & 1
        owner_at = (jnp.where(native, 0, 4) + (owner >> 2)) * 2 + owner_l
        along = jnp.broadcast_to(owner_at, (128, 128))
        alike = jnp.where((along == along.T) & earlier, 1, 0)
        position = jnp.sum(alike, axis=0, keepdims=True)
        is_mine = owner_at == group_at
        columns = (
            slot,
            owner_at * 64 + block_at * 4 + (position >> 2),
            position & 3,
            block_at * 16 + (token >> 3),
            token & 7,
            jnp.where(is_mine, slot - role_col * 4, -1),
            jnp.where(is_mine, block_at * 4 + (position >> 2), -1),
            token,
        )
        for j, column in enumerate(columns):
            out[i, j : j + 1, :] = column


def matching(row_count, row_period, column_count, column_period, shift=0):
    row = lax.broadcasted_iota(jnp.int32, (row_count, column_count), 0) & (row_period - 1)
    column = lax.broadcasted_iota(jnp.int32, (row_count, column_count), 1) & (column_period - 1)
    return (row - shift == column).astype(jnp.bfloat16)


def places(ints, i, first=0):
    across = jnp.concatenate([ints[first + 2 * i], ints[first + 2 * i + 1]], axis=1)
    return across.T, across


def rank_kernel(first, shrink, ints, *refs):
    shards, (out, rows, sems) = refs[:-3], refs[-3:]
    for i, shard in enumerate(shards):
        pltpu.make_async_copy(shard, rows.at[pl.ds(i * 128, 128)], sems.at[i * 128 // TILE]).start()
    out[...] = jnp.zeros(out.shape, jnp.float32)
    fold = matching(128, 32, 128, 32)

    def tile(i, carry):
        part = pl.ds(pl.multiple_of(i * TILE, TILE), TILE)
        down, across = places(ints, i, first)
        pltpu.make_async_copy(rows.at[part], rows.at[part], sems.at[i]).wait()
        group = lanes(TILE, 128, 32)
        values = kept(group == down[:, 5:6], contract_trailing(rows[part, :], shrink[...]))
        values = kept(group == down[:, 2:3], dot(values, fold))
        place = lax.broadcasted_iota(jnp.int32, (64, TILE), 0) == across[6:7]
        out[...] += dot(place.astype(jnp.bfloat16), values)
        return carry

    lax.fori_loop(0, rows.shape[0] // TILE, tile, 0)


def hidden_kernel(first, slab_at, ranks, ints, expand, down_shrink, *refs):
    shards, pieces, (hidden, packed, rows, weight, to_gate, to_up, fold, row_sems, sem) = refs[:8], refs[8:16], refs[16:]
    slab = pieces[0].shape[0]
    for i, piece in enumerate(pieces):
        start = pl.multiple_of(slab_at[i] * slab, 128)
        pltpu.make_async_copy(piece, weight.at[pl.ds(start, slab)], sem.at[0]).start()
    for i, shard in enumerate(shards):
        pltpu.make_async_copy(shard, rows.at[pl.ds(i * 128, 128)], row_sems.at[i * 128 // TILE]).start()
    packed[...] = jnp.zeros(packed.shape, jnp.float32)
    to_gate[...] = matching(128, 32, 1024, 16)
    to_up[...] = matching(128, 32, 1024, 16, 16)
    fold[...] = matching(1024, 16, 128, 16)
    units = hidden.shape[1]

    def tile(i, carry):
        part = pl.ds(pl.multiple_of(i * TILE, TILE), TILE)
        down, across = places(ints, i, first)
        place = lanes(TILE, ranks.shape[0], 1) == down[:, 1:2]
        own = kept(lanes(TILE, 128, 32) == down[:, 2:3], dot(place.astype(jnp.bfloat16), ranks[...]))
        chosen = lanes(TILE, to_gate.shape[1], 16) == down[:, 0:1]
        gate = dot(kept(chosen, dot(own, to_gate[...])), expand[0])
        up = dot(kept(chosen, dot(own, to_up[...])), expand[1])
        pltpu.make_async_copy(rows.at[part], rows.at[part], row_sems.at[i]).wait()

        @pl.when(i == 0)
        def _():
            pltpu.make_async_copy(weight, weight, sem.at[0]).wait()

        both = dot(rows[part, :], weight[...])
        gate, up = gate + both[:, :units], up + both[:, units:]
        values = (gate / (1.0 + jnp.exp(-gate)) * up).astype(jnp.bfloat16)
        hidden[part, :] = values
        parts = dot(kept(chosen, contract_trailing(values, down_shrink[...])), fold[...])
        parts = kept(lanes(TILE, 128, 16) == down[:, 4:5], parts)
        place = lax.broadcasted_iota(jnp.int32, (packed.shape[0], TILE), 0) == across[3:4]
        packed[...] += dot(place.astype(jnp.bfloat16), parts)
        return carry

    lax.fori_loop(0, rows.shape[0] // TILE, tile, 0)


def down_kernel(slab_at, hidden, *refs):
    pieces, (mine, theirs, weight, sems) = refs[:8], refs[8:]
    slab, step = pieces[0].shape[1], pl.program_id(0)

    @pl.when(step == 0)
    def _():
        for i, piece in enumerate(pieces):
            start = pl.multiple_of((slab_at[i] & 1) * slab, 128)
            chunk = slab_at[i] >> 1
            pltpu.make_async_copy(piece, weight.at[chunk, :, pl.ds(start, slab)], sems.at[chunk]).start()

    pltpu.make_async_copy(weight.at[step], weight.at[step], sems.at[step]).wait()
    both = dot(hidden[...], weight[step]).astype(jnp.bfloat16)
    mine[...] = both[:TILE]
    theirs[...] = both[TILE:]


def adapter_kernel(ranks, ints, lane_slot, *refs):
    maps, (mine, theirs, whole, sem) = refs[:8], refs[8:]
    for i, piece in enumerate(maps):
        pltpu.make_async_copy(piece, whole.at[pl.ds(i * 64, 64)], sem.at[0]).start()
    spread = matching(128, 16, 512, 16)
    pltpu.make_async_copy(whole, whole, sem.at[0]).wait()
    for t, out in enumerate((mine, theirs)):
        down = ints[ROW_BLOCKS.index(8 * t)].T
        place = lanes(128, 16, 1) == down[:, 7:8] >> 3
        own = kept(lanes(128, 128, 16) == down[:, 4:5], dot(place.astype(jnp.bfloat16), ranks[t]))
        own = kept(lane_slot[...] == down[:, 0:1], dot(own, spread))
        out[...] = dot(own, whole[...]).astype(jnp.bfloat16)


def weight_blocks(shard, ci):
    other = send(shard, OTHER_ROLE)
    same = jnp.where(ci == 0, shard, send(shard, SAME_ROLE))
    same_low, other_high = send(same, X_UP), send(other, X_DOWN)
    other_low, same_high = send(other, X_UP), send(same, X_DOWN)
    same_far, other_far = send(same_low, X_UP), send(other_high, X_DOWN)
    return [same, same_low, same_high, same_far, other, other_low, other_high, other_far]


def local(
    hidden_states,
    norm_gain,
    gate_base,
    up_base,
    down_base,
    shrink_gu,
    expand_gu,
    down_shrink_maps,
    down_expand_maps,
    token_adapter,
    adapter_slot,
):
    xi, ci, yi, hi, li = (lax.axis_index(name) for name in ALL)
    own_count, width = hidden_states.shape
    units = gate_base.shape[1]
    adapter_list = adapter_slot.shape[0]
    owner_partial = adapter_list // 16
    rank = down_expand_maps.shape[0] // owner_partial
    total = 16 * own_count

    slab_at = [((xi + dx) % 4) * 2 + (ci if half == 0 else 1 - ci) for half in range(2) for dx in X_ORDER]

    slab_at = jnp.stack(slab_at).astype(jnp.int32)

    gate_up = weight_blocks(jnp.concatenate([gate_base, up_base], axis=1), ci)
    mine = [rms_normed(hidden_states, norm_gain)]
    for k in range(7):
        mine.append(send(mine[SOURCE[k]], TREE[k]))
    theirs = [send(block, CORE) for block in mine]
    shards = [(mine + theirs)[k] for k in ROW_BLOCKS]

    shrink = send(shrink_gu, OTHER_ROLE)
    expand = send(expand_gu, OTHER_ROLE)
    down = weight_blocks(down_base, ci)
    down_shrink = send(down_shrink_maps, OTHER_ROLE)
    down_expand = send(down_expand_maps, OTHER_ROLE)

    maps = [down_expand]
    for k in range(7):
        maps.append(send(maps[SOURCE[k]], TREE[k]))

    def pick(table, k):
        return jnp.where(ci == 0, table[0][k], table[1][k])

    map_slots = []
    for k in range(8):
        from_y, from_l = (yi + pick(BLOCK_Y, k)) % 4, (li + pick(BLOCK_L, k)) % 2
        map_slots.append((from_y * 4 + jnp.where(ci == 0, hi * 2 + from_l, 3 - hi * 2 - from_l)) * owner_partial)
    lane_slot = jnp.stack(map_slots).astype(jnp.int32)[:, None] + jnp.arange(64, dtype=jnp.int32)[None, :] // rank
    lane_slot = lane_slot.reshape(1, 512)

    half_count = total // 2
    vmem = pl.BlockSpec(memory_space=pltpu.VMEM)
    smem = pl.BlockSpec(memory_space=pltpu.SMEM)
    stay = pl.BlockSpec(memory_space=pl.ANY)

    own_adapters = token_adapter.reshape(16, own_count)
    ints = pl.pallas_call(
        place_kernel,
        out_shape=jax.ShapeDtypeStruct((16, 8, own_count), jnp.int32),
        in_specs=[smem, smem, vmem, vmem],
        out_specs=vmem,
        scratch_shapes=[pltpu.VMEM((2, 16, own_count), jnp.int32)],
        name="places",
    )(jnp.stack([ci, yi, hi, li]), adapter_slot, own_adapters, send(own_adapters, CORE))

    def ranks_of(first, last):
        count = (last - first) * own_count
        return pl.pallas_call(
            functools.partial(rank_kernel, first),
            out_shape=jax.ShapeDtypeStruct((64, 128), jnp.float32),
            in_specs=[vmem] * 2 + [stay] * (last - first),
            out_specs=vmem,
            scratch_shapes=[
                pltpu.VMEM((count, width), jnp.bfloat16),
                pltpu.SemaphoreType.DMA((count // TILE,)),
            ],
            name="ranks",
        )(shrink, ints, *shards[first:last])

    packed = ranks_of(LATE_BLOCKS, 16) + ranks_of(0, LATE_BLOCKS)
    spread = jnp.broadcast_to(packed.astype(jnp.bfloat16)[None], (16, 64, 128))
    ranks = lax.all_to_all(spread, GROUP, split_axis=0, concat_axis=0, tiled=True).reshape(1024, 128)

    def hidden_half(i):
        return pl.pallas_call(
            functools.partial(hidden_kernel, 8 * i),
            out_shape=(
                jax.ShapeDtypeStruct((half_count, units), jnp.bfloat16),
                jax.ShapeDtypeStruct((256, 128), jnp.float32),
            ),
            in_specs=[smem] + [vmem] * 4 + [stay] * 16,
            out_specs=(vmem, vmem),
            scratch_shapes=[
                pltpu.VMEM((half_count, width), jnp.bfloat16),
                pltpu.VMEM((width, 2 * units), jnp.bfloat16),
                pltpu.VMEM((128, 1024), jnp.bfloat16),
                pltpu.VMEM((128, 1024), jnp.bfloat16),
                pltpu.VMEM((1024, 128), jnp.bfloat16),
                pltpu.SemaphoreType.DMA((half_count // TILE,)),
                pltpu.SemaphoreType.DMA((1,)),
            ],
            name="hidden",
        )(
            slab_at,
            ranks,
            ints,
            expand,
            down_shrink,
            *shards[8 * i : 8 * i + 8],
            *gate_up,
        )

    def down_quarter(hidden, i):
        return pl.pallas_call(
            down_kernel,
            grid=(4,),
            out_shape=(jax.ShapeDtypeStruct((TILE, width), jnp.bfloat16),) * 2,
            in_specs=[smem, pl.BlockSpec((2 * TILE, units), lambda g: (i, 0))] + [stay] * 8,
            out_specs=(pl.BlockSpec((TILE, width // 4), lambda g: (0, g)),) * 2,
            scratch_shapes=[pltpu.VMEM((4, units, width // 4), jnp.bfloat16), pltpu.SemaphoreType.DMA((4,))],
            name="down",
        )(slab_at, hidden, *down)

    def add(left, right):
        return (left.astype(jnp.float32) + right.astype(jnp.float32)).astype(jnp.bfloat16)

    sums = [None] * 8
    packed_down = []
    for i in range(2):
        hidden, packed = hidden_half(i)
        packed_down.append(packed)
        for j in range(2):
            mine_part, theirs_part = down_quarter(hidden, j)
            swapped = send(theirs_part, CORE)
            added = [add(mine_part[at : at + 128], swapped[at : at + 128]) for at in (0, 128)]
            for k, value in zip(HALVES[i][2 * j : 2 * j + 2], lax.optimization_barrier(added)):
                sums[k] = value

    packed_down = (packed_down[0] + packed_down[1]).astype(jnp.bfloat16).reshape(16, 16, 128)
    arrived = lax.all_to_all(packed_down, GROUP, split_axis=0, concat_axis=0, tiled=True)
    down_ranks = jnp.sum(arrived.astype(jnp.float32), axis=0).astype(jnp.bfloat16)
    both_ranks = jnp.stack([down_ranks, send(down_ranks, CORE)])
    own_adapter, their_adapter = pl.pallas_call(
        adapter_kernel,
        out_shape=(jax.ShapeDtypeStruct((own_count, width), jnp.bfloat16),) * 2,
        in_specs=[vmem] * 3 + [stay] * 8,
        out_specs=(vmem, vmem),
        scratch_shapes=[pltpu.VMEM((512, width), jnp.bfloat16), pltpu.SemaphoreType.DMA((1,))],
        name="adapters",
    )(both_ranks, ints, lane_slot, *maps)
    adapter_term = own_adapter.astype(jnp.float32) + send(their_adapter, CORE).astype(jnp.float32)

    for k in (6, 5, 4, 3, 2, 1):
        sums[SOURCE[k]] = add(sums[SOURCE[k]], send(sums[k + 1], TREE_BACK[k]))
    last = send(sums[1], TREE_BACK[0]).astype(jnp.float32)
    near = lax.optimization_barrier(sums[0].astype(jnp.float32) + adapter_term)
    return (near + last).astype(jnp.bfloat16)


def solution(mesh):
    fine = Mesh(mesh.devices.reshape(4, 2, 4, 2, 2), ALL)
    row, col = ("x", "c"), ("y", "h", "l")
    in_specs = (
        P(row + col, None),
        P(),
        P(row, col),
        P(row, col),
        P(col, row),
        P(col, None),
        P(None, None, col),
        P(None, col),
        P(col, None),
        P(row),
        P(),
    )
    out_specs = P(row + col, None)
    return jax.shard_map(local, mesh=fine, in_specs=in_specs, out_specs=out_specs, check_vma=False)
```

```python
import functools

import jax
import jax.numpy as jnp
from jax import lax
from jax.experimental import pallas as pl
from jax.experimental.pallas import tpu as pltpu
from jax.sharding import Mesh, PartitionSpec as P


eps = 1e-05
ALL = ("x", "c", "y", "h", "l")
GROUP = ("c", "y", "l")

SOURCE = (0, 0, 0, 1, 1, 2, 4)
STEPS = (
    (("y", -1), ("y", 1), ("l", 1), ("y", -1), ("l", 1), ("l", 1), ("l", 1)),
    (("l", 1), ("y", 1), ("y", -1), ("y", 1), ("y", -1), ("y", 1), ("y", 1)),
)
BLOCK_Y = ((0, 1, -1, 0, 2, 1, -1, 2), (0, 0, -1, 1, -1, 1, 2, 2))
BLOCK_L = ((0, 0, 0, 1, 0, 1, 1, 1), (0, 1, 0, 0, 1, 1, 0, 1))
X_ORDER = (0, -1, 1, 2)


def flat(x, c, y, z):
    return (((x % 4) * 2 + c % 2) * 4 + y % 4) * 4 + z % 4


def pairs_of(move):
    return [
        (flat(x, c, y, z), flat(*move(x, c, y, z)))
        for x in range(4)
        for c in range(2)
        for y in range(4)
        for z in range(4)
    ]


def tree_pairs(k):
    def move(x, c, y, z):
        axis, shift = STEPS[c][k]
        return (x, c, y + shift, z) if axis == "y" else (x, c, y, z ^ 1)

    return pairs_of(move)


TREE = [tree_pairs(k) for k in range(7)]
TREE_BACK = [[(b, a) for a, b in pairs] for pairs in TREE]
CORE = pairs_of(lambda x, c, y, z: (x, 1 - c, y, z))
SAME_ROLE = [pair for pair in pairs_of(lambda x, c, y, z: (x, c, y, 3 - z)) if pair[0] // 16 % 2 == 1]
OTHER_ROLE = pairs_of(lambda x, c, y, z: (x, 1 - c, y, 3 - z if c == 0 else z))
X_UP = pairs_of(lambda x, c, y, z: (x + 1, c, y, z))
X_DOWN = pairs_of(lambda x, c, y, z: (x - 1, c, y, z))


HALVES = ((7, 6, 5, 4), (3, 2, 1, 0))
ROW_BLOCKS = tuple(
    half[2 * pair + j] + 8 * part for half in HALVES for pair in range(2) for part in range(2) for j in range(2)
)
LATE_BLOCKS = 8
TILE = 256


def send(value, pairs):
    return lax.ppermute(value, ALL, pairs)


def contract_trailing(left, right):
    return lax.dot_general(
        left, right, (((left.ndim - 1,), (1,)), ((), ())), preferred_element_type=jnp.float32
    )


def dot(left, right):
    return jnp.dot(left, right, preferred_element_type=jnp.float32)


def rms_normed(states, norm_gain):
    values = states.astype(jnp.float32)
    scale_inv = lax.rsqrt(jnp.mean(values * values, axis=-1, keepdims=True) + eps)
    return (values * scale_inv * norm_gain).astype(jnp.bfloat16)


def lanes(rows, count, group):
    return lax.broadcasted_iota(jnp.int32, (rows, count), 1) // group


def kept(mask, values):
    return jnp.where(mask, values, 0.0).astype(jnp.bfloat16)


def place_kernel(at, slot_of, own, other, out, slots):
    ci, yi, hi, li = (at[i] for i in range(4))
    for part, adapters in enumerate((own, other)):
        ids = adapters[...]
        found = jnp.zeros(ids.shape, jnp.int32)
        for adapter in range(slot_of.shape[0]):
            found = jnp.where(ids == adapter, slot_of[adapter], found)
        slots[part] = found
    role_col = yi * 4 + jnp.where(ci == 0, hi * 2 + li, 3 - hi * 2 - li)
    group_at = (ci * 4 + yi) * 2 + li
    earlier = lax.broadcasted_iota(jnp.int32, (128, 128), 0) < lax.broadcasted_iota(jnp.int32, (128, 128), 1)
    token = lax.broadcasted_iota(jnp.int32, (1, 128), 1)
    for i, k in enumerate(ROW_BLOCKS):
        part, k = k // 8, k % 8
        c = ci if part == 0 else 1 - ci
        y = (yi + 4 + jnp.where(c == 0, BLOCK_Y[0][k], BLOCK_Y[1][k])) & 3
        l = (li + jnp.where(c == 0, BLOCK_L[0][k], BLOCK_L[1][k])) & 1
        block_at = (c * 4 + y) * 2 + l
        slot = slots[part, pl.ds(y * 4 + hi * 2 + l, 1), :]
        owner = slot >> 2
        owner_z = owner & 3
        native = (owner_z >> 1) == hi
        owner_l = jnp.where(native, owner_z, 3 - owner_z) & 1
        owner_at = (jnp.where(native, 0, 4) + (owner >> 2)) * 2 + owner_l
        along = jnp.broadcast_to(owner_at, (128, 128))
        alike = jnp.where((along == along.T) & earlier, 1, 0)
        position = jnp.sum(alike, axis=0, keepdims=True)
        is_mine = owner_at == group_at
        columns = (
            slot,
            owner_at * 64 + block_at * 4 + (position >> 2),
            position & 3,
            block_at * 16 + (token >> 3),
            token & 7,
            jnp.where(is_mine, slot - role_col * 4, -1),
            jnp.where(is_mine, block_at * 4 + (position >> 2), -1),
            token,
        )
        for j, column in enumerate(columns):
            out[i, j : j + 1, :] = column


def matching(row_count, row_period, column_count, column_period, shift=0):
    row = lax.broadcasted_iota(jnp.int32, (row_count, column_count), 0) & (row_period - 1)
    column = lax.broadcasted_iota(jnp.int32, (row_count, column_count), 1) & (column_period - 1)
    return (row - shift == column).astype(jnp.bfloat16)


def places(ints, i, first=0):
    across = jnp.concatenate([ints[first + 2 * i], ints[first + 2 * i + 1]], axis=1)
    return across.T, across


def rank_kernel(first, shrink, ints, *refs):
    shards, (out, rows, sems) = refs[:-3], refs[-3:]
    for i, shard in enumerate(shards):
        pltpu.make_async_copy(shard, rows.at[pl.ds(i * 128, 128)], sems.at[i * 128 // TILE]).start()
    out[...] = jnp.zeros(out.shape, jnp.float32)
    fold = matching(128, 32, 128, 32)

    def tile(i, carry):
        part = pl.ds(pl.multiple_of(i * TILE, TILE), TILE)
        down, across = places(ints, i, first)
        pltpu.make_async_copy(rows.at[part], rows.at[part], sems.at[i]).wait()
        group = lanes(TILE, 128, 32)
        values = kept(group == down[:, 5:6], contract_trailing(rows[part, :], shrink[...]))
        values = kept(group == down[:, 2:3], dot(values, fold))
        place = lax.broadcasted_iota(jnp.int32, (64, TILE), 0) == across[6:7]
        out[...] += dot(place.astype(jnp.bfloat16), values)
        return carry

    lax.fori_loop(0, rows.shape[0] // TILE, tile, 0)


def hidden_kernel(first, slab_at, ranks, ints, expand, down_shrink, *refs):
    shards, pieces, (hidden, packed, rows, weight, to_gate, to_up, fold, row_sems, sem) = refs[:8], refs[8:16], refs[16:]
    slab = pieces[0].shape[0]
    for i, piece in enumerate(pieces):
        start = pl.multiple_of(slab_at[i] * slab, 128)
        pltpu.make_async_copy(piece, weight.at[pl.ds(start, slab)], sem.at[0]).start()
    for i, shard in enumerate(shards):
        pltpu.make_async_copy(shard, rows.at[pl.ds(i * 128, 128)], row_sems.at[i * 128 // TILE]).start()
    packed[...] = jnp.zeros(packed.shape, jnp.float32)
    to_gate[...] = matching(128, 32, 1024, 16)
    to_up[...] = matching(128, 32, 1024, 16, 16)
    fold[...] = matching(1024, 16, 128, 16)
    units = hidden.shape[1]

    def tile(i, carry):
        part = pl.ds(pl.multiple_of(i * TILE, TILE), TILE)
        down, across = places(ints, i, first)
        place = lanes(TILE, ranks.shape[0], 1) == down[:, 1:2]
        own = kept(lanes(TILE, 128, 32) == down[:, 2:3], dot(place.astype(jnp.bfloat16), ranks[...]))
        chosen = lanes(TILE, to_gate.shape[1], 16) == down[:, 0:1]
        gate = dot(kept(chosen, dot(own, to_gate[...])), expand[0])
        up = dot(kept(chosen, dot(own, to_up[...])), expand[1])
        pltpu.make_async_copy(rows.at[part], rows.at[part], row_sems.at[i]).wait()

        @pl.when(i == 0)
        def _():
            pltpu.make_async_copy(weight, weight, sem.at[0]).wait()

        both = dot(rows[part, :], weight[...])
        gate, up = gate + both[:, :units], up + both[:, units:]
        values = (gate / (1.0 + jnp.exp(-gate)) * up).astype(jnp.bfloat16)
        hidden[part, :] = values
        parts = dot(kept(chosen, contract_trailing(values, down_shrink[...])), fold[...])
        parts = kept(lanes(TILE, 128, 16) == down[:, 4:5], parts)
        place = lax.broadcasted_iota(jnp.int32, (packed.shape[0], TILE), 0) == across[3:4]
        packed[...] += dot(place.astype(jnp.bfloat16), parts)
        return carry

    lax.fori_loop(0, rows.shape[0] // TILE, tile, 0)


def down_kernel(slab_at, hidden, *refs):
    pieces, (mine, theirs, weight, sems) = refs[:8], refs[8:]
    slab, step = pieces[0].shape[1], pl.program_id(0)

    @pl.when(step == 0)
    def _():
        for i, piece in enumerate(pieces):
            start = pl.multiple_of((slab_at[i] & 1) * slab, 128)
            chunk = slab_at[i] >> 1
            pltpu.make_async_copy(piece, weight.at[chunk, :, pl.ds(start, slab)], sems.at[chunk]).start()

    pltpu.make_async_copy(weight.at[step], weight.at[step], sems.at[step]).wait()
    both = dot(hidden[...], weight[step]).astype(jnp.bfloat16)
    mine[...] = both[:TILE]
    theirs[...] = both[TILE:]


def adapter_kernel(map_slots, ranks, ints, *refs):
    maps, (mine, theirs, whole, sem) = refs[:8], refs[8:]
    for i, piece in enumerate(maps):
        pltpu.make_async_copy(piece, whole.at[pl.ds(i * 64, 64)], sem.at[0]).start()
    spread = matching(128, 16, 512, 16)
    lane = lax.broadcasted_iota(jnp.int32, (1, 512), 1)
    first = jnp.zeros((1, 512), jnp.int32)
    for i in range(8):
        first = jnp.where(lane >> 6 == i, map_slots[i], first)
    lane_slot = first + ((lane >> 4) & 3)
    pltpu.make_async_copy(whole, whole, sem.at[0]).wait()
    for t, out in enumerate((mine, theirs)):
        down = ints[ROW_BLOCKS.index(8 * t)].T
        place = lanes(128, 16, 1) == down[:, 7:8] >> 3
        own = kept(lanes(128, 128, 16) == down[:, 4:5], dot(place.astype(jnp.bfloat16), ranks[t]))
        own = kept(lane_slot == down[:, 0:1], dot(own, spread))
        out[...] = dot(own, whole[...]).astype(jnp.bfloat16)


def weight_blocks(shard, ci):
    other = send(shard, OTHER_ROLE)
    same = jnp.where(ci == 0, shard, send(shard, SAME_ROLE))
    same_low, other_high = send(same, X_UP), send(other, X_DOWN)
    other_low, same_high = send(other, X_UP), send(same, X_DOWN)
    same_far, other_far = send(same_low, X_UP), send(other_high, X_DOWN)
    return [same, same_low, same_high, same_far, other, other_low, other_high, other_far]


def local(
    hidden_states,
    norm_gain,
    gate_base,
    up_base,
    down_base,
    shrink_gu,
    expand_gu,
    down_shrink_maps,
    down_expand_maps,
    token_adapter,
    adapter_slot,
):
    xi, ci, yi, hi, li = (lax.axis_index(name) for name in ALL)
    own_count, width = hidden_states.shape
    units = gate_base.shape[1]
    adapter_list = adapter_slot.shape[0]
    owner_partial = adapter_list // 16
    total = 16 * own_count

    slab_at = [((xi + dx) % 4) * 2 + (ci if half == 0 else 1 - ci) for half in range(2) for dx in X_ORDER]

    slab_at = jnp.stack(slab_at).astype(jnp.int32)

    gate_up = weight_blocks(jnp.concatenate([gate_base, up_base], axis=1), ci)
    mine = [rms_normed(hidden_states, norm_gain)]
    for k in range(7):
        mine.append(send(mine[SOURCE[k]], TREE[k]))
    theirs = [send(block, CORE) for block in mine]
    shards = [(mine + theirs)[k] for k in ROW_BLOCKS]

    shrink = send(shrink_gu, OTHER_ROLE)
    expand = send(expand_gu, OTHER_ROLE)
    down = weight_blocks(down_base, ci)
    down_shrink = send(down_shrink_maps, OTHER_ROLE)
    down_expand = send(down_expand_maps, OTHER_ROLE)

    maps = [down_expand]
    for k in range(7):
        maps.append(send(maps[SOURCE[k]], TREE[k]))

    def pick(table, k):
        return jnp.where(ci == 0, table[0][k], table[1][k])

    map_slots = []
    for k in range(8):
        from_y, from_l = (yi + pick(BLOCK_Y, k)) % 4, (li + pick(BLOCK_L, k)) % 2
        map_slots.append((from_y * 4 + jnp.where(ci == 0, hi * 2 + from_l, 3 - hi * 2 - from_l)) * owner_partial)
    map_slots = jnp.stack(map_slots).astype(jnp.int32)

    half_count = total // 2
    vmem = pl.BlockSpec(memory_space=pltpu.VMEM)
    smem = pl.BlockSpec(memory_space=pltpu.SMEM)
    stay = pl.BlockSpec(memory_space=pl.ANY)

    own_adapters = token_adapter.reshape(16, own_count)
    ints = pl.pallas_call(
        place_kernel,
        out_shape=jax.ShapeDtypeStruct((16, 8, own_count), jnp.int32),
        in_specs=[smem, smem, vmem, vmem],
        out_specs=vmem,
        scratch_shapes=[pltpu.VMEM((2, 16, own_count), jnp.int32)],
        name="places",
    )(jnp.stack([ci, yi, hi, li]), adapter_slot, own_adapters, send(own_adapters, CORE))

    def ranks_of(first, last):
        count = (last - first) * own_count
        return pl.pallas_call(
            functools.partial(rank_kernel, first),
            out_shape=jax.ShapeDtypeStruct((64, 128), jnp.float32),
            in_specs=[vmem] * 2 + [stay] * (last - first),
            out_specs=vmem,
            scratch_shapes=[
                pltpu.VMEM((count, width), jnp.bfloat16),
                pltpu.SemaphoreType.DMA((count // TILE,)),
            ],
            name="ranks",
        )(shrink, ints, *shards[first:last])

    packed = ranks_of(LATE_BLOCKS, 16) + ranks_of(0, LATE_BLOCKS)
    spread = jnp.broadcast_to(packed.astype(jnp.bfloat16)[None], (16, 64, 128))
    ranks = lax.all_to_all(spread, GROUP, split_axis=0, concat_axis=0, tiled=True).reshape(1024, 128)

    def hidden_half(i):
        return pl.pallas_call(
            functools.partial(hidden_kernel, 8 * i),
            out_shape=(
                jax.ShapeDtypeStruct((half_count, units), jnp.bfloat16),
                jax.ShapeDtypeStruct((256, 128), jnp.float32),
            ),
            in_specs=[smem] + [vmem] * 4 + [stay] * 16,
            out_specs=(vmem, vmem),
            scratch_shapes=[
                pltpu.VMEM((half_count, width), jnp.bfloat16),
                pltpu.VMEM((width, 2 * units), jnp.bfloat16),
                pltpu.VMEM((128, 1024), jnp.bfloat16),
                pltpu.VMEM((128, 1024), jnp.bfloat16),
                pltpu.VMEM((1024, 128), jnp.bfloat16),
                pltpu.SemaphoreType.DMA((half_count // TILE,)),
                pltpu.SemaphoreType.DMA((1,)),
            ],
            name="hidden",
        )(
            slab_at,
            ranks,
            ints,
            expand,
            down_shrink,
            *shards[8 * i : 8 * i + 8],
            *gate_up,
        )

    def down_quarter(hidden, i):
        return pl.pallas_call(
            down_kernel,
            grid=(4,),
            out_shape=(jax.ShapeDtypeStruct((TILE, width), jnp.bfloat16),) * 2,
            in_specs=[smem, pl.BlockSpec((2 * TILE, units), lambda g: (i, 0))] + [stay] * 8,
            out_specs=(pl.BlockSpec((TILE, width // 4), lambda g: (0, g)),) * 2,
            scratch_shapes=[pltpu.VMEM((4, units, width // 4), jnp.bfloat16), pltpu.SemaphoreType.DMA((4,))],
            name="down",
        )(slab_at, hidden, *down)

    def add(left, right):
        return (left.astype(jnp.float32) + right.astype(jnp.float32)).astype(jnp.bfloat16)

    sums = [None] * 8
    packed_down = []
    for i in range(2):
        hidden, packed = hidden_half(i)
        packed_down.append(packed)
        for j in range(2):
            mine_part, theirs_part = down_quarter(hidden, j)
            swapped = send(theirs_part, CORE)
            added = [add(mine_part[at : at + 128], swapped[at : at + 128]) for at in (0, 128)]
            for k, value in zip(HALVES[i][2 * j : 2 * j + 2], lax.optimization_barrier(added)):
                sums[k] = value

    packed_down = (packed_down[0] + packed_down[1]).astype(jnp.bfloat16).reshape(16, 16, 128)
    arrived = lax.all_to_all(packed_down, GROUP, split_axis=0, concat_axis=0, tiled=True)
    down_ranks = jnp.sum(arrived.astype(jnp.float32), axis=0).astype(jnp.bfloat16)
    both_ranks = jnp.stack([down_ranks, send(down_ranks, CORE)])
    own_adapter, their_adapter = pl.pallas_call(
        adapter_kernel,
        out_shape=(jax.ShapeDtypeStruct((own_count, width), jnp.bfloat16),) * 2,
        in_specs=[smem] + [vmem] * 2 + [stay] * 8,
        out_specs=(vmem, vmem),
        scratch_shapes=[pltpu.VMEM((512, width), jnp.bfloat16), pltpu.SemaphoreType.DMA((1,))],
        name="adapters",
    )(map_slots, both_ranks, ints, *maps)
    adapter_term = own_adapter.astype(jnp.float32) + send(their_adapter, CORE).astype(jnp.float32)

    for k in (6, 5, 4, 3, 2, 1):
        sums[SOURCE[k]] = add(sums[SOURCE[k]], send(sums[k + 1], TREE_BACK[k]))
    last = send(sums[1], TREE_BACK[0]).astype(jnp.float32)
    near = lax.optimization_barrier(sums[0].astype(jnp.float32) + adapter_term)
    return (near + last).astype(jnp.bfloat16)


def solution(mesh):
    fine = Mesh(mesh.devices.reshape(4, 2, 4, 2, 2), ALL)
    row, col = ("x", "c"), ("y", "h", "l")
    in_specs = (
        P(row + col, None),
        P(),
        P(row, col),
        P(row, col),
        P(col, row),
        P(col, None),
        P(None, None, col),
        P(None, col),
        P(col, None),
        P(row),
        P(),
    )
    out_specs = P(row + col, None)
    return jax.shard_map(local, mesh=fine, in_specs=in_specs, out_specs=out_specs, check_vma=False)
```

```python
import functools

import jax
import jax.numpy as jnp
from jax import lax
from jax.experimental import pallas as pl
from jax.experimental.pallas import tpu as pltpu
from jax.sharding import Mesh, PartitionSpec as P


eps = 1e-05
ALL = ("x", "c", "y", "h", "l")
GROUP = ("c", "y", "l")

SOURCE = (0, 0, 0, 1, 1, 2, 4)
STEPS = (
    (("y", -1), ("y", 1), ("l", 1), ("y", -1), ("l", 1), ("l", 1), ("l", 1)),
    (("l", 1), ("y", 1), ("y", -1), ("y", 1), ("y", -1), ("y", 1), ("y", 1)),
)
BLOCK_Y = ((0, 1, -1, 0, 2, 1, -1, 2), (0, 0, -1, 1, -1, 1, 2, 2))
BLOCK_L = ((0, 0, 0, 1, 0, 1, 1, 1), (0, 1, 0, 0, 1, 1, 0, 1))
X_ORDER = (0, -1, 1, 2)


def flat(x, c, y, z):
    return (((x % 4) * 2 + c % 2) * 4 + y % 4) * 4 + z % 4


def pairs_of(move):
    return [
        (flat(x, c, y, z), flat(*move(x, c, y, z)))
        for x in range(4)
        for c in range(2)
        for y in range(4)
        for z in range(4)
    ]


def tree_pairs(k):
    def move(x, c, y, z):
        axis, shift = STEPS[c][k]
        return (x, c, y + shift, z) if axis == "y" else (x, c, y, z ^ 1)

    return pairs_of(move)


TREE = [tree_pairs(k) for k in range(7)]
TREE_BACK = [[(b, a) for a, b in pairs] for pairs in TREE]
CORE = pairs_of(lambda x, c, y, z: (x, 1 - c, y, z))
SAME_ROLE = [pair for pair in pairs_of(lambda x, c, y, z: (x, c, y, 3 - z)) if pair[0] // 16 % 2 == 1]
OTHER_ROLE = pairs_of(lambda x, c, y, z: (x, 1 - c, y, 3 - z if c == 0 else z))
X_UP = pairs_of(lambda x, c, y, z: (x + 1, c, y, z))
X_DOWN = pairs_of(lambda x, c, y, z: (x - 1, c, y, z))


HALVES = ((7, 6, 5, 4), (3, 2, 1, 0))
ROW_BLOCKS = tuple(k + 8 * part for half in HALVES for part in range(2) for k in half)
LATE_BLOCKS = 8
TILE = 256


def send(value, pairs):
    return lax.ppermute(value, ALL, pairs)


def contract_trailing(left, right):
    return lax.dot_general(
        left, right, (((left.ndim - 1,), (1,)), ((), ())), preferred_element_type=jnp.float32
    )


def dot(left, right):
    return jnp.dot(left, right, preferred_element_type=jnp.float32)


def rms_normed(states, norm_gain):
    values = states.astype(jnp.float32)
    scale_inv = lax.rsqrt(jnp.mean(values * values, axis=-1, keepdims=True) + eps)
    return (values * scale_inv * norm_gain).astype(jnp.bfloat16)


def lanes(rows, count, group):
    return lax.broadcasted_iota(jnp.int32, (rows, count), 1) // group


def kept(mask, values):
    return jnp.where(mask, values, 0.0).astype(jnp.bfloat16)


def place_kernel(at, slot_of, own, other, out, slots):
    ci, yi, hi, li = (at[i] for i in range(4))
    for part, adapters in enumerate((own, other)):
        ids = adapters[...]
        found = jnp.zeros(ids.shape, jnp.int32)
        for adapter in range(slot_of.shape[0]):
            found = jnp.where(ids == adapter, slot_of[adapter], found)
        slots[part] = found
    role_col = yi * 4 + jnp.where(ci == 0, hi * 2 + li, 3 - hi * 2 - li)
    group_at = (ci * 4 + yi) * 2 + li
    earlier = lax.broadcasted_iota(jnp.int32, (128, 128), 0) < lax.broadcasted_iota(jnp.int32, (128, 128), 1)
    token = lax.broadcasted_iota(jnp.int32, (1, 128), 1)
    for i, k in enumerate(ROW_BLOCKS):
        part, k = k // 8, k % 8
        c = ci if part == 0 else 1 - ci
        y = (yi + 4 + jnp.where(c == 0, BLOCK_Y[0][k], BLOCK_Y[1][k])) & 3
        l = (li + jnp.where(c == 0, BLOCK_L[0][k], BLOCK_L[1][k])) & 1
        block_at = (c * 4 + y) * 2 + l
        slot = slots[part, pl.ds(y * 4 + hi * 2 + l, 1), :]
        owner = slot >> 2
        owner_z = owner & 3
        native = (owner_z >> 1) == hi
        owner_l = jnp.where(native, owner_z, 3 - owner_z) & 1
        owner_at = (jnp.where(native, 0, 4) + (owner >> 2)) * 2 + owner_l
        along = jnp.broadcast_to(owner_at, (128, 128))
        alike = jnp.where((along == along.T) & earlier, 1, 0)
        position = jnp.sum(alike, axis=0, keepdims=True)
        is_mine = owner_at == group_at
        columns = (
            slot,
            owner_at * 64 + block_at * 4 + (position >> 2),
            position & 3,
            block_at * 16 + (token >> 3),
            token & 7,
            jnp.where(is_mine, slot - role_col * 4, -1),
            jnp.where(is_mine, block_at * 4 + (position >> 2), -1),
            token,
        )
        for j, column in enumerate(columns):
            out[i, j : j + 1, :] = column


def matching(row_count, row_period, column_count, column_period, shift=0):
    row = lax.broadcasted_iota(jnp.int32, (row_count, column_count), 0) & (row_period - 1)
    column = lax.broadcasted_iota(jnp.int32, (row_count, column_count), 1) & (column_period - 1)
    return (row - shift == column).astype(jnp.bfloat16)


def places(ints, i, first=0):
    across = jnp.concatenate([ints[first + 2 * i], ints[first + 2 * i + 1]], axis=1)
    return across.T, across


def rank_kernel(first, shrink, ints, before, *refs):
    shards, (out, total, rows, sems) = refs[:-4], refs[-4:]
    for i, shard in enumerate(shards):
        pltpu.make_async_copy(shard, rows.at[pl.ds(i * 128, 128)], sems.at[i * 128 // TILE]).start()
    total[...] = before[...]
    fold = matching(128, 32, 128, 32)

    def tile(i, carry):
        part = pl.ds(pl.multiple_of(i * TILE, TILE), TILE)
        down, across = places(ints, i, first)
        pltpu.make_async_copy(rows.at[part], rows.at[part], sems.at[i]).wait()
        group = lanes(TILE, 128, 32)
        values = kept(group == down[:, 5:6], contract_trailing(rows[part, :], shrink[...]))
        values = kept(group == down[:, 2:3], dot(values, fold))
        place = lax.broadcasted_iota(jnp.int32, (64, TILE), 0) == across[6:7]
        total[...] += dot(place.astype(jnp.bfloat16), values)
        return carry

    lax.fori_loop(0, rows.shape[0] // TILE, tile, 0)
    out[...] = jnp.broadcast_to(total[...].astype(out.dtype), out.shape)


def hidden_kernel(first, slab_at, ranks, ints, expand, down_shrink, before, *refs):
    shards, pieces, (hidden, packed, total, rows, weight, to_gate, to_up, fold, row_sems, sem) = refs[:8], refs[8:16], refs[16:]
    slab = pieces[0].shape[0]
    for i, piece in enumerate(pieces):
        start = pl.multiple_of(slab_at[i] * slab, 128)
        pltpu.make_async_copy(piece, weight.at[pl.ds(start, slab)], sem.at[0]).start()
    for i, shard in enumerate(shards):
        pltpu.make_async_copy(shard, rows.at[pl.ds(i * 128, 128)], row_sems.at[i * 128 // TILE]).start()
    total[...] = before[...]
    to_gate[...] = matching(128, 32, 1024, 16)
    to_up[...] = matching(128, 32, 1024, 16, 16)
    fold[...] = matching(1024, 16, 128, 16)
    units = hidden.shape[1]

    def tile(i, carry):
        part = pl.ds(pl.multiple_of(i * TILE, TILE), TILE)
        down, across = places(ints, i, first)
        place = lanes(TILE, ranks.shape[0], 1) == down[:, 1:2]
        own = kept(lanes(TILE, 128, 32) == down[:, 2:3], dot(place.astype(jnp.bfloat16), ranks[...]))
        chosen = lanes(TILE, to_gate.shape[1], 16) == down[:, 0:1]
        gate = dot(kept(chosen, dot(own, to_gate[...])), expand[0])
        up = dot(kept(chosen, dot(own, to_up[...])), expand[1])
        pltpu.make_async_copy(rows.at[part], rows.at[part], row_sems.at[i]).wait()

        @pl.when(i == 0)
        def _():
            pltpu.make_async_copy(weight, weight, sem.at[0]).wait()

        both = dot(rows[part, :], weight[...])
        gate, up = gate + both[:, :units], up + both[:, units:]
        values = (gate / (1.0 + jnp.exp(-gate)) * up).astype(jnp.bfloat16)
        hidden[part, :] = values
        parts = dot(kept(chosen, contract_trailing(values, down_shrink[...])), fold[...])
        parts = kept(lanes(TILE, 128, 16) == down[:, 4:5], parts)
        place = lax.broadcasted_iota(jnp.int32, (packed.shape[0], TILE), 0) == across[3:4]
        total[...] += dot(place.astype(jnp.bfloat16), parts)
        return carry

    lax.fori_loop(0, rows.shape[0] // TILE, tile, 0)
    packed[...] = total[...].astype(packed.dtype)


def down_kernel(slab_at, hidden, *refs):
    pieces, (out, weight, sems) = refs[:8], refs[8:]
    slab, step = pieces[0].shape[1], pl.program_id(0)

    @pl.when(step == 0)
    def _():
        for i, piece in enumerate(pieces):
            start = pl.multiple_of((slab_at[i] & 1) * slab, 128)
            chunk = slab_at[i] >> 1
            pltpu.make_async_copy(piece, weight.at[chunk, :, pl.ds(start, slab)], sems.at[chunk]).start()

    pltpu.make_async_copy(weight.at[step], weight.at[step], sems.at[step]).wait()
    out[...] = dot(hidden[...], weight[step]).astype(jnp.bfloat16)


def adapter_kernel(map_slots, ranks, ints, *refs):
    maps, (mine, theirs, whole, sem) = refs[:8], refs[8:]
    for i, piece in enumerate(maps):
        pltpu.make_async_copy(piece, whole.at[pl.ds(i * 64, 64)], sem.at[0]).start()
    spread = matching(128, 16, 512, 16)
    lane = lax.broadcasted_iota(jnp.int32, (1, 512), 1)
    first = jnp.zeros((1, 512), jnp.int32)
    for i in range(8):
        first = jnp.where(lane >> 6 == i, map_slots[i], first)
    lane_slot = first + ((lane >> 4) & 3)
    pltpu.make_async_copy(whole, whole, sem.at[0]).wait()
    for t, out in enumerate((mine, theirs)):
        down = ints[ROW_BLOCKS.index(8 * t)].T
        place = lanes(128, 16, 1) == down[:, 7:8] >> 3
        own = kept(lanes(128, 128, 16) == down[:, 4:5], dot(place.astype(jnp.bfloat16), ranks[t]))
        own = kept(lane_slot == down[:, 0:1], dot(own, spread))
        out[...] = dot(own, whole[...]).astype(jnp.bfloat16)


def weight_blocks(shard, ci):
    other = send(shard, OTHER_ROLE)
    same = jnp.where(ci == 0, shard, send(shard, SAME_ROLE))
    same_low, other_high = send(same, X_UP), send(other, X_DOWN)
    other_low, same_high = send(other, X_UP), send(same, X_DOWN)
    same_far, other_far = send(same_low, X_UP), send(other_high, X_DOWN)
    return [same, same_low, same_high, same_far, other, other_low, other_high, other_far]


def local(
    hidden_states,
    norm_gain,
    gate_base,
    up_base,
    down_base,
    shrink_gu,
    expand_gu,
    down_shrink_maps,
    down_expand_maps,
    token_adapter,
    adapter_slot,
):
    xi, ci, yi, hi, li = (lax.axis_index(name) for name in ALL)
    own_count, width = hidden_states.shape
    units = gate_base.shape[1]
    adapter_list = adapter_slot.shape[0]
    owner_partial = adapter_list // 16
    total = 16 * own_count

    slab_at = [((xi + dx) % 4) * 2 + (ci if half == 0 else 1 - ci) for half in range(2) for dx in X_ORDER]

    slab_at = jnp.stack(slab_at).astype(jnp.int32)

    gate_up = weight_blocks(jnp.concatenate([gate_base, up_base], axis=1), ci)
    mine = [rms_normed(hidden_states, norm_gain)]
    for k in range(7):
        mine.append(send(mine[SOURCE[k]], TREE[k]))
    theirs = [send(block, CORE) for block in mine]
    shards = [(mine + theirs)[k] for k in ROW_BLOCKS]

    shrink = send(shrink_gu, OTHER_ROLE)
    expand = send(expand_gu, OTHER_ROLE)
    down = weight_blocks(down_base, ci)
    down_shrink = send(down_shrink_maps, OTHER_ROLE)
    down_expand = send(down_expand_maps, OTHER_ROLE)

    maps = [down_expand]
    for k in range(7):
        maps.append(send(maps[SOURCE[k]], TREE[k]))

    def pick(table, k):
        return jnp.where(ci == 0, table[0][k], table[1][k])

    map_slots = []
    for k in range(8):
        from_y, from_l = (yi + pick(BLOCK_Y, k)) % 4, (li + pick(BLOCK_L, k)) % 2
        map_slots.append((from_y * 4 + jnp.where(ci == 0, hi * 2 + from_l, 3 - hi * 2 - from_l)) * owner_partial)
    map_slots = jnp.stack(map_slots).astype(jnp.int32)

    half_count = total // 2
    vmem = pl.BlockSpec(memory_space=pltpu.VMEM)
    smem = pl.BlockSpec(memory_space=pltpu.SMEM)
    stay = pl.BlockSpec(memory_space=pl.ANY)

    own_adapters = token_adapter.reshape(16, own_count)
    ints = pl.pallas_call(
        place_kernel,
        out_shape=jax.ShapeDtypeStruct((16, 8, own_count), jnp.int32),
        in_specs=[smem, smem, vmem, vmem],
        out_specs=vmem,
        scratch_shapes=[pltpu.VMEM((2, 16, own_count), jnp.int32)],
        name="places",
    )(jnp.stack([ci, yi, hi, li]), adapter_slot, own_adapters, send(own_adapters, CORE))

    def ranks_of(first, last, before, out_shape):
        count = (last - first) * own_count
        return pl.pallas_call(
            functools.partial(rank_kernel, first),
            out_shape=out_shape,
            in_specs=[vmem] * 3 + [stay] * (last - first),
            out_specs=vmem,
            scratch_shapes=[
                pltpu.VMEM((64, 128), jnp.float32),
                pltpu.VMEM((count, width), jnp.bfloat16),
                pltpu.SemaphoreType.DMA((count // TILE,)),
            ],
            name="ranks",
        )(shrink, ints, before, *shards[first:last])

    packed = jax.ShapeDtypeStruct((64, 128), jnp.float32)
    packed = ranks_of(LATE_BLOCKS, 16, jnp.zeros((64, 128), jnp.float32), packed)
    spread = jax.ShapeDtypeStruct((16, 64, 128), jnp.bfloat16)
    spread = ranks_of(0, LATE_BLOCKS, packed, spread)
    ranks = lax.all_to_all(spread, GROUP, split_axis=0, concat_axis=0, tiled=True).reshape(1024, 128)

    def hidden_half(i, before, kind):
        return pl.pallas_call(
            functools.partial(hidden_kernel, 8 * i),
            out_shape=(jax.ShapeDtypeStruct((half_count, units), jnp.bfloat16), jax.ShapeDtypeStruct((256, 128), kind)),
            in_specs=[smem] + [vmem] * 5 + [stay] * 16,
            out_specs=(vmem, vmem),
            scratch_shapes=[
                pltpu.VMEM((256, 128), jnp.float32),
                pltpu.VMEM((half_count, width), jnp.bfloat16),
                pltpu.VMEM((width, 2 * units), jnp.bfloat16),
                pltpu.VMEM((128, 1024), jnp.bfloat16),
                pltpu.VMEM((128, 1024), jnp.bfloat16),
                pltpu.VMEM((1024, 128), jnp.bfloat16),
                pltpu.SemaphoreType.DMA((half_count // TILE,)),
                pltpu.SemaphoreType.DMA((1,)),
            ],
            name="hidden",
        )(
            slab_at,
            ranks,
            ints,
            expand,
            down_shrink,
            before,
            *shards[8 * i : 8 * i + 8],
            *gate_up,
        )

    def down_part(hidden, i):
        return pl.pallas_call(
            down_kernel,
            grid=(4,),
            out_shape=jax.ShapeDtypeStruct((4 * own_count, width), jnp.bfloat16),
            in_specs=[smem, pl.BlockSpec((4 * own_count, units), lambda g: (i, 0))] + [stay] * 8,
            out_specs=pl.BlockSpec((4 * own_count, width // 4), lambda g: (0, g)),
            scratch_shapes=[pltpu.VMEM((4, units, width // 4), jnp.bfloat16), pltpu.SemaphoreType.DMA((4,))],
            name="down",
        )(slab_at, hidden, *down)

    def add(left, right):
        return (left.astype(jnp.float32) + right.astype(jnp.float32)).astype(jnp.bfloat16)

    sums = [None] * 8
    packed_down = jnp.zeros((256, 128), jnp.float32)
    for i, kind in enumerate((jnp.float32, jnp.bfloat16)):
        hidden, packed_down = hidden_half(i, packed_down, kind)
        swapped = send(down_part(hidden, 1), CORE)
        own_part = down_part(hidden, 0)
        spans = [slice(j * own_count, (j + 1) * own_count) for j in range(4)]
        added = lax.optimization_barrier([add(own_part[span], swapped[span]) for span in spans])
        for k, value in zip(HALVES[i], added):
            sums[k] = value

    packed_down = packed_down.reshape(16, 16, 128)
    arrived = lax.all_to_all(packed_down, GROUP, split_axis=0, concat_axis=0, tiled=True)
    down_ranks = jnp.sum(arrived.astype(jnp.float32), axis=0).astype(jnp.bfloat16)
    both_ranks = jnp.stack([down_ranks, send(down_ranks, CORE)])
    own_adapter, their_adapter = pl.pallas_call(
        adapter_kernel,
        out_shape=(jax.ShapeDtypeStruct((own_count, width), jnp.bfloat16),) * 2,
        in_specs=[smem] + [vmem] * 2 + [stay] * 8,
        out_specs=(vmem, vmem),
        scratch_shapes=[pltpu.VMEM((512, width), jnp.bfloat16), pltpu.SemaphoreType.DMA((1,))],
        name="adapters",
    )(map_slots, both_ranks, ints, *maps)
    adapter_term = own_adapter.astype(jnp.float32) + send(their_adapter, CORE).astype(jnp.float32)

    for k in (6, 5, 4, 3, 2, 1):
        sums[SOURCE[k]] = add(sums[SOURCE[k]], send(sums[k + 1], TREE_BACK[k]))
    last = send(sums[1], TREE_BACK[0]).astype(jnp.float32)
    return (sums[0].astype(jnp.float32) + last + adapter_term).astype(jnp.bfloat16)


def solution(mesh):
    fine = Mesh(mesh.devices.reshape(4, 2, 4, 2, 2), ALL)
    row, col = ("x", "c"), ("y", "h", "l")
    in_specs = (
        P(row + col, None),
        P(),
        P(row, col),
        P(row, col),
        P(col, row),
        P(col, None),
        P(None, None, col),
        P(None, col),
        P(col, None),
        P(row),
        P(),
    )
    out_specs = P(row + col, None)
    return jax.shard_map(local, mesh=fine, in_specs=in_specs, out_specs=out_specs, check_vma=False)
```

```python
import functools

import jax
import jax.numpy as jnp
from jax import lax
from jax.experimental import pallas as pl
from jax.experimental.pallas import tpu as pltpu
from jax.sharding import Mesh, PartitionSpec as P


eps = 1e-05
ALL = ("x", "c", "y", "h", "l")
GROUP = ("c", "y", "l")

SOURCE = (0, 0, 0, 1, 1, 2, 4)
STEPS = (
    (("y", -1), ("y", 1), ("l", 1), ("y", -1), ("l", 1), ("l", 1), ("l", 1)),
    (("l", 1), ("y", 1), ("y", -1), ("y", 1), ("y", -1), ("y", 1), ("y", 1)),
)
BLOCK_Y = ((0, 1, -1, 0, 2, 1, -1, 2), (0, 0, -1, 1, -1, 1, 2, 2))
BLOCK_L = ((0, 0, 0, 1, 0, 1, 1, 1), (0, 1, 0, 0, 1, 1, 0, 1))
X_ORDER = (0, -1, 1, 2)


def flat(x, c, y, z):
    return (((x % 4) * 2 + c % 2) * 4 + y % 4) * 4 + z % 4


def pairs_of(move):
    return [
        (flat(x, c, y, z), flat(*move(x, c, y, z)))
        for x in range(4)
        for c in range(2)
        for y in range(4)
        for z in range(4)
    ]


def tree_pairs(k):
    def move(x, c, y, z):
        axis, shift = STEPS[c][k]
        return (x, c, y + shift, z) if axis == "y" else (x, c, y, z ^ 1)

    return pairs_of(move)


TREE = [tree_pairs(k) for k in range(7)]
TREE_BACK = [[(b, a) for a, b in pairs] for pairs in TREE]
CORE = pairs_of(lambda x, c, y, z: (x, 1 - c, y, z))
SAME_ROLE = [pair for pair in pairs_of(lambda x, c, y, z: (x, c, y, 3 - z)) if pair[0] // 16 % 2 == 1]
OTHER_ROLE = pairs_of(lambda x, c, y, z: (x, 1 - c, y, 3 - z if c == 0 else z))
X_UP = pairs_of(lambda x, c, y, z: (x + 1, c, y, z))
X_DOWN = pairs_of(lambda x, c, y, z: (x - 1, c, y, z))


HALVES = ((7, 6, 5, 4), (3, 2, 1, 0))
ROW_BLOCKS = tuple(
    half[2 * pair + j] + 8 * part for half in HALVES for pair in range(2) for part in range(2) for j in range(2)
)
LATE_BLOCKS = 8
TILE = 256


def send(value, pairs):
    return lax.ppermute(value, ALL, pairs)


def contract_trailing(left, right):
    return lax.dot_general(
        left, right, (((left.ndim - 1,), (1,)), ((), ())), preferred_element_type=jnp.float32
    )


def dot(left, right):
    return jnp.dot(left, right, preferred_element_type=jnp.float32)


def rms_normed(states, norm_gain):
    values = states.astype(jnp.float32)
    scale_inv = lax.rsqrt(jnp.mean(values * values, axis=-1, keepdims=True) + eps)
    return (values * scale_inv * norm_gain).astype(jnp.bfloat16)


def lanes(rows, count, group):
    return lax.broadcasted_iota(jnp.int32, (rows, count), 1) // group


def kept(mask, values):
    return jnp.where(mask, values, 0.0).astype(jnp.bfloat16)


def place_kernel(at, slot_of, own, other, out, slots):
    ci, yi, hi, li = (at[i] for i in range(4))
    for part, adapters in enumerate((own, other)):
        ids = adapters[...]
        found = jnp.zeros(ids.shape, jnp.int32)
        for adapter in range(slot_of.shape[0]):
            found = jnp.where(ids == adapter, slot_of[adapter], found)
        slots[part] = found
    role_col = yi * 4 + jnp.where(ci == 0, hi * 2 + li, 3 - hi * 2 - li)
    group_at = (ci * 4 + yi) * 2 + li
    earlier = lax.broadcasted_iota(jnp.int32, (128, 128), 0) < lax.broadcasted_iota(jnp.int32, (128, 128), 1)
    token = lax.broadcasted_iota(jnp.int32, (1, 128), 1)
    for i, k in enumerate(ROW_BLOCKS):
        part, k = k // 8, k % 8
        c = ci if part == 0 else 1 - ci
        y = (yi + 4 + jnp.where(c == 0, BLOCK_Y[0][k], BLOCK_Y[1][k])) & 3
        l = (li + jnp.where(c == 0, BLOCK_L[0][k], BLOCK_L[1][k])) & 1
        block_at = (c * 4 + y) * 2 + l
        slot = slots[part, pl.ds(y * 4 + hi * 2 + l, 1), :]
        owner = slot >> 2
        owner_z = owner & 3
        native = (owner_z >> 1) == hi
        owner_l = jnp.where(native, owner_z, 3 - owner_z) & 1
        owner_at = (jnp.where(native, 0, 4) + (owner >> 2)) * 2 + owner_l
        along = jnp.broadcast_to(owner_at, (128, 128))
        alike = jnp.where((along == along.T) & earlier, 1, 0)
        position = jnp.sum(alike, axis=0, keepdims=True)
        is_mine = owner_at == group_at
        columns = (
            slot,
            owner_at * 64 + block_at * 4 + (position >> 2),
            position & 3,
            block_at * 16 + (token >> 3),
            token & 7,
            jnp.where(is_mine, slot - role_col * 4, -1),
            jnp.where(is_mine, block_at * 4 + (position >> 2), -1),
            token,
        )
        for j, column in enumerate(columns):
            out[i, j : j + 1, :] = column


def matching(row_count, row_period, column_count, column_period, shift=0):
    row = lax.broadcasted_iota(jnp.int32, (row_count, column_count), 0) & (row_period - 1)
    column = lax.broadcasted_iota(jnp.int32, (row_count, column_count), 1) & (column_period - 1)
    return (row - shift == column).astype(jnp.bfloat16)


def places(ints, i, first=0):
    across = jnp.concatenate([ints[first + 2 * i], ints[first + 2 * i + 1]], axis=1)
    return across.T, across


def rank_kernel(first, shrink, ints, before, *refs):
    shards, (out, total, rows, sems) = refs[:-4], refs[-4:]
    for i, shard in enumerate(shards):
        pltpu.make_async_copy(shard, rows.at[pl.ds(i * 128, 128)], sems.at[i * 128 // TILE]).start()
    total[...] = before[...]
    fold = matching(128, 32, 128, 32)

    def tile(i, carry):
        part = pl.ds(pl.multiple_of(i * TILE, TILE), TILE)
        down, across = places(ints, i, first)
        pltpu.make_async_copy(rows.at[part], rows.at[part], sems.at[i]).wait()
        group = lanes(TILE, 128, 32)
        values = kept(group == down[:, 5:6], contract_trailing(rows[part, :], shrink[...]))
        values = kept(group == down[:, 2:3], dot(values, fold))
        place = lax.broadcasted_iota(jnp.int32, (64, TILE), 0) == across[6:7]
        total[...] += dot(place.astype(jnp.bfloat16), values)
        return carry

    lax.fori_loop(0, rows.shape[0] // TILE, tile, 0)
    out[...] = jnp.broadcast_to(total[...].astype(out.dtype), out.shape)


def hidden_kernel(first, slab_at, ranks, ints, expand, down_shrink, before, *refs):
    shards, pieces, (hidden, packed, total, rows, weight, to_gate, to_up, fold, row_sems, sem) = refs[:8], refs[8:16], refs[16:]
    slab = pieces[0].shape[0]
    for i, piece in enumerate(pieces):
        start = pl.multiple_of(slab_at[i] * slab, 128)
        pltpu.make_async_copy(piece, weight.at[pl.ds(start, slab)], sem.at[0]).start()
    for i, shard in enumerate(shards):
        pltpu.make_async_copy(shard, rows.at[pl.ds(i * 128, 128)], row_sems.at[i * 128 // TILE]).start()
    total[...] = before[...]
    to_gate[...] = matching(128, 32, 1024, 16)
    to_up[...] = matching(128, 32, 1024, 16, 16)
    fold[...] = matching(1024, 16, 128, 16)
    units = hidden.shape[1]

    def tile(i, carry):
        part = pl.ds(pl.multiple_of(i * TILE, TILE), TILE)
        down, across = places(ints, i, first)
        place = lanes(TILE, ranks.shape[0], 1) == down[:, 1:2]
        own = kept(lanes(TILE, 128, 32) == down[:, 2:3], dot(place.astype(jnp.bfloat16), ranks[...]))
        chosen = lanes(TILE, to_gate.shape[1], 16) == down[:, 0:1]
        gate = dot(kept(chosen, dot(own, to_gate[...])), expand[0])
        up = dot(kept(chosen, dot(own, to_up[...])), expand[1])
        pltpu.make_async_copy(rows.at[part], rows.at[part], row_sems.at[i]).wait()

        @pl.when(i == 0)
        def _():
            pltpu.make_async_copy(weight, weight, sem.at[0]).wait()

        both = dot(rows[part, :], weight[...])
        gate, up = gate + both[:, :units], up + both[:, units:]
        values = (gate / (1.0 + jnp.exp(-gate)) * up).astype(jnp.bfloat16)
        hidden[part, :] = values
        parts = dot(kept(chosen, contract_trailing(values, down_shrink[...])), fold[...])
        parts = kept(lanes(TILE, 128, 16) == down[:, 4:5], parts)
        place = lax.broadcasted_iota(jnp.int32, (total.shape[0], TILE), 0) == across[3:4]
        total[...] += dot(place.astype(jnp.bfloat16), parts)
        return carry

    lax.fori_loop(0, rows.shape[0] // TILE, tile, 0)
    packed[...] = total[...].astype(packed.dtype)


def down_kernel(slab_at, hidden, *refs):
    pieces, (mine, theirs, weight, sems) = refs[:8], refs[8:]
    slab, step = pieces[0].shape[1], pl.program_id(0)

    @pl.when(step == 0)
    def _():
        for i, piece in enumerate(pieces):
            start = pl.multiple_of((slab_at[i] & 1) * slab, 128)
            chunk = slab_at[i] >> 1
            pltpu.make_async_copy(piece, weight.at[chunk, :, pl.ds(start, slab)], sems.at[chunk]).start()

    pltpu.make_async_copy(weight.at[step], weight.at[step], sems.at[step]).wait()
    both = dot(hidden[...], weight[step]).astype(jnp.bfloat16)
    mine[...] = both[:TILE]
    theirs[...] = both[TILE:]


def adapter_kernel(map_slots, ranks, ints, *refs):
    maps, (mine, theirs, whole, sem) = refs[:8], refs[8:]
    for i, piece in enumerate(maps):
        pltpu.make_async_copy(piece, whole.at[pl.ds(i * 64, 64)], sem.at[0]).start()
    spread = matching(128, 16, 512, 16)
    lane = lax.broadcasted_iota(jnp.int32, (1, 512), 1)
    first = jnp.zeros((1, 512), jnp.int32)
    for i in range(8):
        first = jnp.where(lane >> 6 == i, map_slots[i], first)
    lane_slot = first + ((lane >> 4) & 3)
    pltpu.make_async_copy(whole, whole, sem.at[0]).wait()
    for t, out in enumerate((mine, theirs)):
        down = ints[ROW_BLOCKS.index(8 * t)].T
        place = lanes(128, 16, 1) == down[:, 7:8] >> 3
        own = kept(lanes(128, 128, 16) == down[:, 4:5], dot(place.astype(jnp.bfloat16), ranks[t]))
        own = kept(lane_slot == down[:, 0:1], dot(own, spread))
        out[...] = dot(own, whole[...]).astype(jnp.bfloat16)


def weight_blocks(shard, ci):
    other = send(shard, OTHER_ROLE)
    same = jnp.where(ci == 0, shard, send(shard, SAME_ROLE))
    same_low, other_high = send(same, X_UP), send(other, X_DOWN)
    other_low, same_high = send(other, X_UP), send(same, X_DOWN)
    same_far, other_far = send(same_low, X_UP), send(other_high, X_DOWN)
    return [same, same_low, same_high, same_far, other, other_low, other_high, other_far]


def local(
    hidden_states,
    norm_gain,
    gate_base,
    up_base,
    down_base,
    shrink_gu,
    expand_gu,
    down_shrink_maps,
    down_expand_maps,
    token_adapter,
    adapter_slot,
):
    xi, ci, yi, hi, li = (lax.axis_index(name) for name in ALL)
    own_count, width = hidden_states.shape
    units = gate_base.shape[1]
    adapter_list = adapter_slot.shape[0]
    owner_partial = adapter_list // 16
    total = 16 * own_count

    slab_at = [((xi + dx) % 4) * 2 + (ci if half == 0 else 1 - ci) for half in range(2) for dx in X_ORDER]

    slab_at = jnp.stack(slab_at).astype(jnp.int32)

    gate_up = weight_blocks(jnp.concatenate([gate_base, up_base], axis=1), ci)
    mine = [rms_normed(hidden_states, norm_gain)]
    for k in range(7):
        mine.append(send(mine[SOURCE[k]], TREE[k]))
    theirs = [send(block, CORE) for block in mine]
    shards = [(mine + theirs)[k] for k in ROW_BLOCKS]

    shrink = send(shrink_gu, OTHER_ROLE)
    expand = send(expand_gu, OTHER_ROLE)
    down = weight_blocks(down_base, ci)
    down_shrink = send(down_shrink_maps, OTHER_ROLE)
    down_expand = send(down_expand_maps, OTHER_ROLE)

    maps = [down_expand]
    for k in range(7):
        maps.append(send(maps[SOURCE[k]], TREE[k]))

    def pick(table, k):
        return jnp.where(ci == 0, table[0][k], table[1][k])

    map_slots = []
    for k in range(8):
        from_y, from_l = (yi + pick(BLOCK_Y, k)) % 4, (li + pick(BLOCK_L, k)) % 2
        map_slots.append((from_y * 4 + jnp.where(ci == 0, hi * 2 + from_l, 3 - hi * 2 - from_l)) * owner_partial)
    map_slots = jnp.stack(map_slots).astype(jnp.int32)

    half_count = total // 2
    vmem = pl.BlockSpec(memory_space=pltpu.VMEM)
    smem = pl.BlockSpec(memory_space=pltpu.SMEM)
    stay = pl.BlockSpec(memory_space=pl.ANY)

    own_adapters = token_adapter.reshape(16, own_count)
    ints = pl.pallas_call(
        place_kernel,
        out_shape=jax.ShapeDtypeStruct((16, 8, own_count), jnp.int32),
        in_specs=[smem, smem, vmem, vmem],
        out_specs=vmem,
        scratch_shapes=[pltpu.VMEM((2, 16, own_count), jnp.int32)],
        name="places",
    )(jnp.stack([ci, yi, hi, li]), adapter_slot, own_adapters, send(own_adapters, CORE))

    def ranks_of(first, last, before, out_shape):
        count = (last - first) * own_count
        return pl.pallas_call(
            functools.partial(rank_kernel, first),
            out_shape=out_shape,
            in_specs=[vmem] * 3 + [stay] * (last - first),
            out_specs=vmem,
            scratch_shapes=[
                pltpu.VMEM((64, 128), jnp.float32),
                pltpu.VMEM((count, width), jnp.bfloat16),
                pltpu.SemaphoreType.DMA((count // TILE,)),
            ],
            name="ranks",
        )(shrink, ints, before, *shards[first:last])

    packed = jax.ShapeDtypeStruct((64, 128), jnp.float32)
    packed = ranks_of(LATE_BLOCKS, 16, jnp.zeros((64, 128), jnp.float32), packed)
    spread = jax.ShapeDtypeStruct((16, 64, 128), jnp.bfloat16)
    spread = ranks_of(0, LATE_BLOCKS, packed, spread)
    ranks = lax.all_to_all(spread, GROUP, split_axis=0, concat_axis=0, tiled=True).reshape(1024, 128)

    def hidden_half(i, before, kind):
        return pl.pallas_call(
            functools.partial(hidden_kernel, 8 * i),
            out_shape=(jax.ShapeDtypeStruct((half_count, units), jnp.bfloat16), jax.ShapeDtypeStruct((256, 128), kind)),
            in_specs=[smem] + [vmem] * 5 + [stay] * 16,
            out_specs=(vmem, vmem),
            scratch_shapes=[
                pltpu.VMEM((256, 128), jnp.float32),
                pltpu.VMEM((half_count, width), jnp.bfloat16),
                pltpu.VMEM((width, 2 * units), jnp.bfloat16),
                pltpu.VMEM((128, 1024), jnp.bfloat16),
                pltpu.VMEM((128, 1024), jnp.bfloat16),
                pltpu.VMEM((1024, 128), jnp.bfloat16),
                pltpu.SemaphoreType.DMA((half_count // TILE,)),
                pltpu.SemaphoreType.DMA((1,)),
            ],
            name="hidden",
        )(
            slab_at,
            ranks,
            ints,
            expand,
            down_shrink,
            before,
            *shards[8 * i : 8 * i + 8],
            *gate_up,
        )

    def down_quarter(hidden, i):
        return pl.pallas_call(
            down_kernel,
            grid=(4,),
            out_shape=(jax.ShapeDtypeStruct((TILE, width), jnp.bfloat16),) * 2,
            in_specs=[smem, pl.BlockSpec((2 * TILE, units), lambda g: (i, 0))] + [stay] * 8,
            out_specs=(pl.BlockSpec((TILE, width // 4), lambda g: (0, g)),) * 2,
            scratch_shapes=[pltpu.VMEM((4, units, width // 4), jnp.bfloat16), pltpu.SemaphoreType.DMA((4,))],
            name="down",
        )(slab_at, hidden, *down)

    def add(left, right):
        return (left.astype(jnp.float32) + right.astype(jnp.float32)).astype(jnp.bfloat16)

    sums = [None] * 8
    packed_down = jnp.zeros((256, 128), jnp.float32)
    for i, kind in enumerate((jnp.float32, jnp.bfloat16)):
        hidden, packed_down = hidden_half(i, packed_down, kind)
        for j in range(2):
            mine_part, theirs_part = down_quarter(hidden, j)
            swapped = send(theirs_part, CORE)
            added = [add(mine_part[at : at + 128], swapped[at : at + 128]) for at in (0, 128)]
            for k, value in zip(HALVES[i][2 * j : 2 * j + 2], lax.optimization_barrier(added)):
                sums[k] = value

    packed_down = packed_down.reshape(16, 16, 128)
    arrived = lax.all_to_all(packed_down, GROUP, split_axis=0, concat_axis=0, tiled=True)
    down_ranks = jnp.sum(arrived.astype(jnp.float32), axis=0).astype(jnp.bfloat16)
    both_ranks = jnp.stack([down_ranks, send(down_ranks, CORE)])
    own_adapter, their_adapter = pl.pallas_call(
        adapter_kernel,
        out_shape=(jax.ShapeDtypeStruct((own_count, width), jnp.bfloat16),) * 2,
        in_specs=[smem] + [vmem] * 2 + [stay] * 8,
        out_specs=(vmem, vmem),
        scratch_shapes=[pltpu.VMEM((512, width), jnp.bfloat16), pltpu.SemaphoreType.DMA((1,))],
        name="adapters",
    )(map_slots, both_ranks, ints, *maps)
    adapter_term = own_adapter.astype(jnp.float32) + send(their_adapter, CORE).astype(jnp.float32)

    for k in (6, 5, 4, 3, 2, 1):
        sums[SOURCE[k]] = add(sums[SOURCE[k]], send(sums[k + 1], TREE_BACK[k]))
    last = send(sums[1], TREE_BACK[0]).astype(jnp.float32)
    return (sums[0].astype(jnp.float32) + last + adapter_term).astype(jnp.bfloat16)


def solution(mesh):
    fine = Mesh(mesh.devices.reshape(4, 2, 4, 2, 2), ALL)
    row, col = ("x", "c"), ("y", "h", "l")
    in_specs = (
        P(row + col, None),
        P(),
        P(row, col),
        P(row, col),
        P(col, row),
        P(col, None),
        P(None, None, col),
        P(None, col),
        P(col, None),
        P(row),
        P(),
    )
    out_specs = P(row + col, None)
    return jax.shard_map(local, mesh=fine, in_specs=in_specs, out_specs=out_specs, check_vma=False)
```

```python
import functools

import jax
import jax.numpy as jnp
from jax import lax
from jax.experimental import pallas as pl
from jax.experimental.pallas import tpu as pltpu
from jax.sharding import Mesh, PartitionSpec as P


eps = 1e-05
ALL = ("x", "c", "y", "h", "l")
GROUP = ("c", "y", "l")

SOURCE = (0, 0, 0, 1, 1, 2, 4)
STEPS = (
    (("y", -1), ("y", 1), ("l", 1), ("y", -1), ("l", 1), ("l", 1), ("l", 1)),
    (("l", 1), ("y", 1), ("y", -1), ("y", 1), ("y", -1), ("y", 1), ("y", 1)),
)
BLOCK_Y = ((0, 1, -1, 0, 2, 1, -1, 2), (0, 0, -1, 1, -1, 1, 2, 2))
BLOCK_L = ((0, 0, 0, 1, 0, 1, 1, 1), (0, 1, 0, 0, 1, 1, 0, 1))
X_ORDER = (0, -1, 1, 2)


def flat(x, c, y, z):
    return (((x % 4) * 2 + c % 2) * 4 + y % 4) * 4 + z % 4


def pairs_of(move):
    return [
        (flat(x, c, y, z), flat(*move(x, c, y, z)))
        for x in range(4)
        for c in range(2)
        for y in range(4)
        for z in range(4)
    ]


def tree_pairs(k):
    def move(x, c, y, z):
        axis, shift = STEPS[c][k]
        return (x, c, y + shift, z) if axis == "y" else (x, c, y, z ^ 1)

    return pairs_of(move)


TREE = [tree_pairs(k) for k in range(7)]
TREE_BACK = [[(b, a) for a, b in pairs] for pairs in TREE]
CORE = pairs_of(lambda x, c, y, z: (x, 1 - c, y, z))
SAME_ROLE = [pair for pair in pairs_of(lambda x, c, y, z: (x, c, y, 3 - z)) if pair[0] // 16 % 2 == 1]
OTHER_ROLE = pairs_of(lambda x, c, y, z: (x, 1 - c, y, 3 - z if c == 0 else z))
X_UP = pairs_of(lambda x, c, y, z: (x + 1, c, y, z))
X_DOWN = pairs_of(lambda x, c, y, z: (x - 1, c, y, z))


HALVES = ((7, 6, 5, 4), (3, 2, 1, 0))
ROW_BLOCKS = tuple(
    half[2 * pair + j] + 8 * part for half in HALVES for pair in range(2) for part in range(2) for j in range(2)
)
LATE_BLOCKS = 8
TILE = 256
RANK_TILE = 512


def send(value, pairs):
    return lax.ppermute(value, ALL, pairs)


def contract_trailing(left, right):
    return lax.dot_general(
        left, right, (((left.ndim - 1,), (1,)), ((), ())), preferred_element_type=jnp.float32
    )


def dot(left, right):
    return jnp.dot(left, right, preferred_element_type=jnp.float32)


def rms_normed(states, norm_gain):
    values = states.astype(jnp.float32)
    scale_inv = lax.rsqrt(jnp.mean(values * values, axis=-1, keepdims=True) + eps)
    return (values * scale_inv * norm_gain).astype(jnp.bfloat16)


def lanes(rows, count, group):
    return lax.broadcasted_iota(jnp.int32, (rows, count), 1) // group


def kept(mask, values):
    return jnp.where(mask, values, 0.0).astype(jnp.bfloat16)


def place_kernel(at, slot_of, own, other, out, slots):
    ci, yi, hi, li = (at[i] for i in range(4))
    for part, adapters in enumerate((own, other)):
        ids = adapters[...]
        found = jnp.zeros(ids.shape, jnp.int32)
        for adapter in range(slot_of.shape[0]):
            found = jnp.where(ids == adapter, slot_of[adapter], found)
        slots[part] = found
    role_col = yi * 4 + jnp.where(ci == 0, hi * 2 + li, 3 - hi * 2 - li)
    group_at = (ci * 4 + yi) * 2 + li
    earlier = lax.broadcasted_iota(jnp.int32, (128, 128), 0) < lax.broadcasted_iota(jnp.int32, (128, 128), 1)
    token = lax.broadcasted_iota(jnp.int32, (1, 128), 1)
    for i, k in enumerate(ROW_BLOCKS):
        part, k = k // 8, k % 8
        c = ci if part == 0 else 1 - ci
        y = (yi + 4 + jnp.where(c == 0, BLOCK_Y[0][k], BLOCK_Y[1][k])) & 3
        l = (li + jnp.where(c == 0, BLOCK_L[0][k], BLOCK_L[1][k])) & 1
        block_at = (c * 4 + y) * 2 + l
        slot = slots[part, pl.ds(y * 4 + hi * 2 + l, 1), :]
        owner = slot >> 2
        owner_z = owner & 3
        native = (owner_z >> 1) == hi
        owner_l = jnp.where(native, owner_z, 3 - owner_z) & 1
        owner_at = (jnp.where(native, 0, 4) + (owner >> 2)) * 2 + owner_l
        along = jnp.broadcast_to(owner_at, (128, 128))
        alike = jnp.where((along == along.T) & earlier, 1, 0)
        position = jnp.sum(alike, axis=0, keepdims=True)
        is_mine = owner_at == group_at
        columns = (
            slot,
            owner_at * 64 + block_at * 4 + (position >> 2),
            position & 3,
            block_at * 16 + (token >> 3),
            token & 7,
            jnp.where(is_mine, slot - role_col * 4, -1),
            jnp.where(is_mine, block_at * 4 + (position >> 2), -1),
            token,
        )
        for j, column in enumerate(columns):
            out[i, j : j + 1, :] = column


def matching(row_count, row_period, column_count, column_period, shift=0):
    row = lax.broadcasted_iota(jnp.int32, (row_count, column_count), 0) & (row_period - 1)
    column = lax.broadcasted_iota(jnp.int32, (row_count, column_count), 1) & (column_period - 1)
    return (row - shift == column).astype(jnp.bfloat16)


def places(ints, i, first=0, count=2):
    across = jnp.concatenate([ints[first + count * i + j] for j in range(count)], axis=1)
    return across.T, across


def rank_kernel(first, shrink, ints, before, *refs):
    shards, (out, total, rows, sems) = refs[:-4], refs[-4:]
    for i, shard in enumerate(shards):
        pltpu.make_async_copy(shard, rows.at[pl.ds(i * 128, 128)], sems.at[i * 128 // RANK_TILE]).start()
    total[...] = before[0:64, :]
    fold = matching(128, 32, 128, 32)

    def tile(i, carry):
        part = pl.ds(pl.multiple_of(i * RANK_TILE, RANK_TILE), RANK_TILE)
        down, across = places(ints, i, first, 4)
        pltpu.make_async_copy(rows.at[part], rows.at[part], sems.at[i]).wait()
        group = lanes(RANK_TILE, 128, 32)
        values = kept(group == down[:, 5:6], contract_trailing(rows[part, :], shrink[...]))
        values = kept(group == down[:, 2:3], dot(values, fold))
        place = lax.broadcasted_iota(jnp.int32, (64, RANK_TILE), 0) == across[6:7]
        total[...] += dot(place.astype(jnp.bfloat16), values)
        return carry

    lax.fori_loop(0, rows.shape[0] // RANK_TILE, tile, 0)
    out[...] = jnp.broadcast_to(total[...].astype(out.dtype), out.shape)


def hidden_kernel(first, slab_at, ranks, ints, expand, down_shrink, before, *refs):
    shards, pieces, (hidden, packed, total, rows, weight, to_gate, to_up, fold, row_sems, sem) = refs[:8], refs[8:16], refs[16:]
    slab = pieces[0].shape[0]
    for i, piece in enumerate(pieces):
        start = pl.multiple_of(slab_at[i] * slab, 128)
        pltpu.make_async_copy(piece, weight.at[pl.ds(start, slab)], sem.at[0]).start()
    for i, shard in enumerate(shards):
        pltpu.make_async_copy(shard, rows.at[pl.ds(i * 128, 128)], row_sems.at[i * 128 // TILE]).start()
    total[...] = before[...]
    to_gate[...] = matching(128, 32, 1024, 16)
    to_up[...] = matching(128, 32, 1024, 16, 16)
    fold[...] = matching(1024, 16, 128, 16)
    units = hidden.shape[1]

    def tile(i, carry):
        part = pl.ds(pl.multiple_of(i * TILE, TILE), TILE)
        down, across = places(ints, i, first)
        place = lanes(TILE, ranks.shape[0], 1) == down[:, 1:2]
        own = kept(lanes(TILE, 128, 32) == down[:, 2:3], dot(place.astype(jnp.bfloat16), ranks[...]))
        chosen = lanes(TILE, to_gate.shape[1], 16) == down[:, 0:1]
        gate = dot(kept(chosen, dot(own, to_gate[...])), expand[0])
        up = dot(kept(chosen, dot(own, to_up[...])), expand[1])
        pltpu.make_async_copy(rows.at[part], rows.at[part], row_sems.at[i]).wait()

        @pl.when(i == 0)
        def _():
            pltpu.make_async_copy(weight, weight, sem.at[0]).wait()

        both = dot(rows[part, :], weight[...])
        gate, up = gate + both[:, :units], up + both[:, units:]
        values = (gate / (1.0 + jnp.exp(-gate)) * up).astype(jnp.bfloat16)
        hidden[part, :] = values
        parts = dot(kept(chosen, contract_trailing(values, down_shrink[...])), fold[...])
        parts = kept(lanes(TILE, 128, 16) == down[:, 4:5], parts)
        place = lax.broadcasted_iota(jnp.int32, (total.shape[0], TILE), 0) == across[3:4]
        total[...] += dot(place.astype(jnp.bfloat16), parts)
        return carry

    lax.fori_loop(0, rows.shape[0] // TILE, tile, 0)
    packed[...] = total[...].astype(packed.dtype)


def down_kernel(slab_at, hidden, *refs):
    pieces, (mine, theirs, weight, sems) = refs[:8], refs[8:]
    slab, step = pieces[0].shape[1], pl.program_id(0)

    @pl.when(step == 0)
    def _():
        for i, piece in enumerate(pieces):
            start = pl.multiple_of((slab_at[i] & 1) * slab, 128)
            chunk = slab_at[i] >> 1
            pltpu.make_async_copy(piece, weight.at[chunk, :, pl.ds(start, slab)], sems.at[chunk]).start()

    pltpu.make_async_copy(weight.at[step], weight.at[step], sems.at[step]).wait()
    both = dot(hidden[...], weight[step]).astype(jnp.bfloat16)
    mine[...] = both[:TILE]
    theirs[...] = both[TILE:]


def adapter_kernel(map_slots, ranks, ints, *refs):
    maps, (mine, theirs, whole, sem) = refs[:8], refs[8:]
    for i, piece in enumerate(maps):
        pltpu.make_async_copy(piece, whole.at[pl.ds(i * 64, 64)], sem.at[0]).start()
    spread = matching(128, 16, 512, 16)
    lane = lax.broadcasted_iota(jnp.int32, (1, 512), 1)
    first = jnp.zeros((1, 512), jnp.int32)
    for i in range(8):
        first = jnp.where(lane >> 6 == i, map_slots[i], first)
    lane_slot = first + ((lane >> 4) & 3)
    pltpu.make_async_copy(whole, whole, sem.at[0]).wait()
    for t, out in enumerate((mine, theirs)):
        down = ints[ROW_BLOCKS.index(8 * t)].T
        place = lanes(128, 16, 1) == down[:, 7:8] >> 3
        own = kept(lanes(128, 128, 16) == down[:, 4:5], dot(place.astype(jnp.bfloat16), ranks[t]))
        own = kept(lane_slot == down[:, 0:1], dot(own, spread))
        out[...] = dot(own, whole[...]).astype(jnp.bfloat16)


def weight_blocks(shard, ci):
    other = send(shard, OTHER_ROLE)
    same = jnp.where(ci == 0, shard, send(shard, SAME_ROLE))
    same_low, other_high = send(same, X_UP), send(other, X_DOWN)
    other_low, same_high = send(other, X_UP), send(same, X_DOWN)
    same_far, other_far = send(same_low, X_UP), send(other_high, X_DOWN)
    return [same, same_low, same_high, same_far, other, other_low, other_high, other_far]


def local(
    hidden_states,
    norm_gain,
    gate_base,
    up_base,
    down_base,
    shrink_gu,
    expand_gu,
    down_shrink_maps,
    down_expand_maps,
    token_adapter,
    adapter_slot,
):
    xi, ci, yi, hi, li = (lax.axis_index(name) for name in ALL)
    own_count, width = hidden_states.shape
    units = gate_base.shape[1]
    adapter_list = adapter_slot.shape[0]
    owner_partial = adapter_list // 16
    total = 16 * own_count

    slab_at = [((xi + dx) % 4) * 2 + (ci if half == 0 else 1 - ci) for half in range(2) for dx in X_ORDER]

    slab_at = jnp.stack(slab_at).astype(jnp.int32)

    gate_up = weight_blocks(jnp.concatenate([gate_base, up_base], axis=1), ci)
    mine = [rms_normed(hidden_states, norm_gain)]
    for k in range(7):
        mine.append(send(mine[SOURCE[k]], TREE[k]))
    theirs = [send(block, CORE) for block in mine]
    shards = [(mine + theirs)[k] for k in ROW_BLOCKS]

    shrink = send(shrink_gu, OTHER_ROLE)
    expand = send(expand_gu, OTHER_ROLE)
    down = weight_blocks(down_base, ci)
    down_shrink = send(down_shrink_maps, OTHER_ROLE)
    down_expand = send(down_expand_maps, OTHER_ROLE)

    maps = [down_expand]
    for k in range(7):
        maps.append(send(maps[SOURCE[k]], TREE[k]))

    def pick(table, k):
        return jnp.where(ci == 0, table[0][k], table[1][k])

    map_slots = []
    for k in range(8):
        from_y, from_l = (yi + pick(BLOCK_Y, k)) % 4, (li + pick(BLOCK_L, k)) % 2
        map_slots.append((from_y * 4 + jnp.where(ci == 0, hi * 2 + from_l, 3 - hi * 2 - from_l)) * owner_partial)
    map_slots = jnp.stack(map_slots).astype(jnp.int32)

    half_count = total // 2
    vmem = pl.BlockSpec(memory_space=pltpu.VMEM)
    smem = pl.BlockSpec(memory_space=pltpu.SMEM)
    stay = pl.BlockSpec(memory_space=pl.ANY)

    own_adapters = token_adapter.reshape(16, own_count)
    ints = pl.pallas_call(
        place_kernel,
        out_shape=jax.ShapeDtypeStruct((16, 8, own_count), jnp.int32),
        in_specs=[smem, smem, vmem, vmem],
        out_specs=vmem,
        scratch_shapes=[pltpu.VMEM((2, 16, own_count), jnp.int32)],
        name="places",
    )(jnp.stack([ci, yi, hi, li]), adapter_slot, own_adapters, send(own_adapters, CORE))

    def ranks_of(first, last, before, out_shape):
        count = (last - first) * own_count
        return pl.pallas_call(
            functools.partial(rank_kernel, first),
            out_shape=out_shape,
            in_specs=[vmem] * 3 + [stay] * (last - first),
            out_specs=vmem,
            scratch_shapes=[
                pltpu.VMEM((64, 128), jnp.float32),
                pltpu.VMEM((count, width), jnp.bfloat16),
                pltpu.SemaphoreType.DMA((count // RANK_TILE,)),
            ],
            name="ranks",
        )(shrink, ints, before, *shards[first:last])

    nothing = jnp.zeros((256, 128), jnp.float32)
    packed = jax.ShapeDtypeStruct((64, 128), jnp.float32)
    packed = ranks_of(LATE_BLOCKS, 16, nothing, packed)
    spread = jax.ShapeDtypeStruct((16, 64, 128), jnp.bfloat16)
    spread = ranks_of(0, LATE_BLOCKS, packed, spread)
    ranks = lax.all_to_all(spread, GROUP, split_axis=0, concat_axis=0, tiled=True).reshape(1024, 128)

    def hidden_half(i, before, kind):
        return pl.pallas_call(
            functools.partial(hidden_kernel, 8 * i),
            out_shape=(jax.ShapeDtypeStruct((half_count, units), jnp.bfloat16), jax.ShapeDtypeStruct((256, 128), kind)),
            in_specs=[smem] + [vmem] * 5 + [stay] * 16,
            out_specs=(vmem, vmem),
            scratch_shapes=[
                pltpu.VMEM((256, 128), jnp.float32),
                pltpu.VMEM((half_count, width), jnp.bfloat16),
                pltpu.VMEM((width, 2 * units), jnp.bfloat16),
                pltpu.VMEM((128, 1024), jnp.bfloat16),
                pltpu.VMEM((128, 1024), jnp.bfloat16),
                pltpu.VMEM((1024, 128), jnp.bfloat16),
                pltpu.SemaphoreType.DMA((half_count // TILE,)),
                pltpu.SemaphoreType.DMA((1,)),
            ],
            name="hidden",
        )(
            slab_at,
            ranks,
            ints,
            expand,
            down_shrink,
            before,
            *shards[8 * i : 8 * i + 8],
            *gate_up,
        )

    def down_quarter(hidden, i):
        return pl.pallas_call(
            down_kernel,
            grid=(4,),
            out_shape=(jax.ShapeDtypeStruct((TILE, width), jnp.bfloat16),) * 2,
            in_specs=[smem, pl.BlockSpec((2 * TILE, units), lambda g: (i, 0))] + [stay] * 8,
            out_specs=(pl.BlockSpec((TILE, width // 4), lambda g: (0, g)),) * 2,
            scratch_shapes=[pltpu.VMEM((4, units, width // 4), jnp.bfloat16), pltpu.SemaphoreType.DMA((4,))],
            name="down",
        )(slab_at, hidden, *down)

    def add(left, right):
        return (left.astype(jnp.float32) + right.astype(jnp.float32)).astype(jnp.bfloat16)

    sums = [None] * 8
    packed_down = nothing
    for i, kind in enumerate((jnp.float32, jnp.bfloat16)):
        hidden, packed_down = hidden_half(i, packed_down, kind)
        for j in range(2):
            mine_part, theirs_part = down_quarter(hidden, j)
            swapped = send(theirs_part, CORE)
            added = [add(mine_part[at : at + 128], swapped[at : at + 128]) for at in (0, 128)]
            for k, value in zip(HALVES[i][2 * j : 2 * j + 2], lax.optimization_barrier(added)):
                sums[k] = value

    packed_down = packed_down.reshape(16, 16, 128)
    arrived = lax.all_to_all(packed_down, GROUP, split_axis=0, concat_axis=0, tiled=True)
    down_ranks = jnp.sum(arrived.astype(jnp.float32), axis=0).astype(jnp.bfloat16)
    both_ranks = jnp.stack([down_ranks, send(down_ranks, CORE)])
    own_adapter, their_adapter = pl.pallas_call(
        adapter_kernel,
        out_shape=(jax.ShapeDtypeStruct((own_count, width), jnp.bfloat16),) * 2,
        in_specs=[smem] + [vmem] * 2 + [stay] * 8,
        out_specs=(vmem, vmem),
        scratch_shapes=[pltpu.VMEM((512, width), jnp.bfloat16), pltpu.SemaphoreType.DMA((1,))],
        name="adapters",
    )(map_slots, both_ranks, ints, *maps)
    adapter_term = own_adapter.astype(jnp.float32) + send(their_adapter, CORE).astype(jnp.float32)

    for k in (6, 5, 4, 3, 2, 1):
        sums[SOURCE[k]] = add(sums[SOURCE[k]], send(sums[k + 1], TREE_BACK[k]))
    last = send(sums[1], TREE_BACK[0]).astype(jnp.float32)
    return (sums[0].astype(jnp.float32) + last + adapter_term).astype(jnp.bfloat16)


def solution(mesh):
    fine = Mesh(mesh.devices.reshape(4, 2, 4, 2, 2), ALL)
    row, col = ("x", "c"), ("y", "h", "l")
    in_specs = (
        P(row + col, None),
        P(),
        P(row, col),
        P(row, col),
        P(col, row),
        P(col, None),
        P(None, None, col),
        P(None, col),
        P(col, None),
        P(row),
        P(),
    )
    out_specs = P(row + col, None)
    return jax.shard_map(local, mesh=fine, in_specs=in_specs, out_specs=out_specs, check_vma=False)
```

```python
import functools

import jax
import jax.numpy as jnp
from jax import lax
from jax.experimental import pallas as pl
from jax.experimental.pallas import tpu as pltpu
from jax.sharding import Mesh, PartitionSpec as P


eps = 1e-05
ALL = ("x", "c", "y", "h", "l")
GROUP = ("c", "y", "l")

SOURCE = (0, 0, 0, 1, 1, 2, 4)
STEPS = (
    (("y", -1), ("y", 1), ("l", 1), ("y", -1), ("l", 1), ("l", 1), ("l", 1)),
    (("l", 1), ("y", 1), ("y", -1), ("y", 1), ("y", -1), ("y", 1), ("y", 1)),
)
BLOCK_Y = ((0, 1, -1, 0, 2, 1, -1, 2), (0, 0, -1, 1, -1, 1, 2, 2))
BLOCK_L = ((0, 0, 0, 1, 0, 1, 1, 1), (0, 1, 0, 0, 1, 1, 0, 1))
X_ORDER = (0, -1, 1, 2)


def flat(x, c, y, z):
    return (((x % 4) * 2 + c % 2) * 4 + y % 4) * 4 + z % 4


def pairs_of(move):
    return [
        (flat(x, c, y, z), flat(*move(x, c, y, z)))
        for x in range(4)
        for c in range(2)
        for y in range(4)
        for z in range(4)
    ]


def tree_pairs(k):
    def move(x, c, y, z):
        axis, shift = STEPS[c][k]
        return (x, c, y + shift, z) if axis == "y" else (x, c, y, z ^ 1)

    return pairs_of(move)


TREE = [tree_pairs(k) for k in range(7)]
TREE_BACK = [[(b, a) for a, b in pairs] for pairs in TREE]
CORE = pairs_of(lambda x, c, y, z: (x, 1 - c, y, z))
SAME_ROLE = [pair for pair in pairs_of(lambda x, c, y, z: (x, c, y, 3 - z)) if pair[0] // 16 % 2 == 1]
OTHER_ROLE = pairs_of(lambda x, c, y, z: (x, 1 - c, y, 3 - z if c == 0 else z))
X_UP = pairs_of(lambda x, c, y, z: (x + 1, c, y, z))
X_DOWN = pairs_of(lambda x, c, y, z: (x - 1, c, y, z))


HALVES = ((7, 6, 5, 4), (3, 2, 1, 0))
ROW_BLOCKS = tuple(
    half[2 * pair + j] + 8 * part for half in HALVES for pair in range(2) for part in range(2) for j in range(2)
)
LATE_BLOCKS = 8
TILE = 256


def send(value, pairs):
    return lax.ppermute(value, ALL, pairs)


def contract_trailing(left, right):
    return lax.dot_general(
        left, right, (((left.ndim - 1,), (1,)), ((), ())), preferred_element_type=jnp.float32
    )


def dot(left, right):
    return jnp.dot(left, right, preferred_element_type=jnp.float32)


def rms_normed(states, norm_gain):
    values = states.astype(jnp.float32)
    scale_inv = lax.rsqrt(jnp.mean(values * values, axis=-1, keepdims=True) + eps)
    return (values * scale_inv * norm_gain).astype(jnp.bfloat16)


def lanes(rows, count, group):
    return lax.broadcasted_iota(jnp.int32, (rows, count), 1) // group


def kept(mask, values):
    return jnp.where(mask, values, 0.0).astype(jnp.bfloat16)


def place_kernel(at, slot_of, own, other, out, slots):
    ci, yi, hi, li = (at[i] for i in range(4))
    for part, adapters in enumerate((own, other)):
        ids = adapters[...]
        found = jnp.zeros(ids.shape, jnp.int32)
        for adapter in range(slot_of.shape[0]):
            found = jnp.where(ids == adapter, slot_of[adapter], found)
        slots[part] = found
    role_col = yi * 4 + jnp.where(ci == 0, hi * 2 + li, 3 - hi * 2 - li)
    group_at = (ci * 4 + yi) * 2 + li
    earlier = lax.broadcasted_iota(jnp.int32, (128, 128), 0) < lax.broadcasted_iota(jnp.int32, (128, 128), 1)
    token = lax.broadcasted_iota(jnp.int32, (1, 128), 1)
    for i, k in enumerate(ROW_BLOCKS):
        part, k = k // 8, k % 8
        c = ci if part == 0 else 1 - ci
        y = (yi + 4 + jnp.where(c == 0, BLOCK_Y[0][k], BLOCK_Y[1][k])) & 3
        l = (li + jnp.where(c == 0, BLOCK_L[0][k], BLOCK_L[1][k])) & 1
        block_at = (c * 4 + y) * 2 + l
        slot = slots[part, pl.ds(y * 4 + hi * 2 + l, 1), :]
        owner = slot >> 2
        owner_z = owner & 3
        native = (owner_z >> 1) == hi
        owner_l = jnp.where(native, owner_z, 3 - owner_z) & 1
        owner_at = (jnp.where(native, 0, 4) + (owner >> 2)) * 2 + owner_l
        along = jnp.broadcast_to(owner_at, (128, 128))
        alike = jnp.where((along == along.T) & earlier, 1, 0)
        position = jnp.sum(alike, axis=0, keepdims=True)
        is_mine = owner_at == group_at
        columns = (
            slot,
            owner_at * 64 + block_at * 4 + (position >> 2),
            position & 3,
            block_at * 16 + (token >> 3),
            token & 7,
            jnp.where(is_mine, slot - role_col * 4, -1),
            jnp.where(is_mine, block_at * 4 + (position >> 2), -1),
            token,
        )
        for j, column in enumerate(columns):
            out[i, j : j + 1, :] = column


def matching(row_count, row_period, column_count, column_period, shift=0):
    row = lax.broadcasted_iota(jnp.int32, (row_count, column_count), 0) & (row_period - 1)
    column = lax.broadcasted_iota(jnp.int32, (row_count, column_count), 1) & (column_period - 1)
    return (row - shift == column).astype(jnp.bfloat16)


def places(ints, i, first=0, count=2):
    across = jnp.concatenate([ints[first + count * i + j] for j in range(count)], axis=1)
    return across.T, across


def rank_kernel(first, shrink, ints, before, *refs):
    shards, (out, total, rows, sems) = refs[:-4], refs[-4:]
    for i, shard in enumerate(shards):
        pltpu.make_async_copy(shard, rows.at[pl.ds(i * 128, 128)], sems.at[i * 128 // TILE]).start()
    total[...] = before[0:64, :]
    fold = matching(128, 32, 128, 32)

    def tile(i, carry):
        part = pl.ds(pl.multiple_of(i * TILE, TILE), TILE)
        down, across = places(ints, i, first)
        pltpu.make_async_copy(rows.at[part], rows.at[part], sems.at[i]).wait()
        group = lanes(TILE, 128, 32)
        values = kept(group == down[:, 5:6], contract_trailing(rows[part, :], shrink[...]))
        values = kept(group == down[:, 2:3], dot(values, fold))
        place = lax.broadcasted_iota(jnp.int32, (64, TILE), 0) == across[6:7]
        total[...] += dot(place.astype(jnp.bfloat16), values)
        return carry

    lax.fori_loop(0, rows.shape[0] // TILE, tile, 0)
    out[...] = jnp.broadcast_to(total[...].astype(out.dtype), out.shape)


def hidden_kernel(first, slab_at, ranks, ints, expand, down_shrink, before, *refs):
    shards, pieces, (hidden, packed, total, rows, weight, to_gate, to_up, fold, row_sems, sem) = refs[:8], refs[8:16], refs[16:]
    slab = pieces[0].shape[0]
    for i, piece in enumerate(pieces):
        start = pl.multiple_of(slab_at[i] * slab, 128)
        pltpu.make_async_copy(piece, weight.at[pl.ds(start, slab)], sem.at[0]).start()
    for i, shard in enumerate(shards):
        pltpu.make_async_copy(shard, rows.at[pl.ds(i * 128, 128)], row_sems.at[i * 128 // TILE]).start()
    total[...] = before[...]
    to_gate[...] = matching(128, 32, 1024, 16)
    to_up[...] = matching(128, 32, 1024, 16, 16)
    fold[...] = matching(1024, 16, 128, 16)
    units = hidden.shape[1]

    def tile(i, carry):
        part = pl.ds(pl.multiple_of(i * TILE, TILE), TILE)
        down, across = places(ints, i, first)
        place = lanes(TILE, ranks.shape[0], 1) == down[:, 1:2]
        own = kept(lanes(TILE, 128, 32) == down[:, 2:3], dot(place.astype(jnp.bfloat16), ranks[...]))
        chosen = lanes(TILE, to_gate.shape[1], 16) == down[:, 0:1]
        gate = dot(kept(chosen, dot(own, to_gate[...])), expand[0])
        up = dot(kept(chosen, dot(own, to_up[...])), expand[1])
        pltpu.make_async_copy(rows.at[part], rows.at[part], row_sems.at[i]).wait()

        @pl.when(i == 0)
        def _():
            pltpu.make_async_copy(weight, weight, sem.at[0]).wait()

        both = dot(rows[part, :], weight[...])
        gate, up = gate + both[:, :units], up + both[:, units:]
        values = (gate / (1.0 + jnp.exp(-gate)) * up).astype(jnp.bfloat16)
        hidden[part, :] = values
        parts = dot(kept(chosen, contract_trailing(values, down_shrink[...])), fold[...])
        parts = kept(lanes(TILE, 128, 16) == down[:, 4:5], parts)
        place = lax.broadcasted_iota(jnp.int32, (total.shape[0], TILE), 0) == across[3:4]
        total[...] += dot(place.astype(jnp.bfloat16), parts)
        return carry

    lax.fori_loop(0, rows.shape[0] // TILE, tile, 0)
    packed[...] = total[...].astype(packed.dtype)


def down_kernel(slab_at, hidden, *refs):
    pieces, (mine, theirs, weight, sems) = refs[:8], refs[8:]
    slab, step = pieces[0].shape[1], pl.program_id(0)

    @pl.when(step == 0)
    def _():
        for i, piece in enumerate(pieces):
            start = pl.multiple_of((slab_at[i] & 1) * slab, 128)
            chunk = slab_at[i] >> 1
            pltpu.make_async_copy(piece, weight.at[chunk, :, pl.ds(start, slab)], sems.at[chunk]).start()

    pltpu.make_async_copy(weight.at[step], weight.at[step], sems.at[step]).wait()
    both = dot(hidden[...], weight[step]).astype(jnp.bfloat16)
    mine[...] = both[:TILE]
    theirs[...] = both[TILE:]


def adapter_kernel(map_slots, ranks, ints, *refs):
    maps, (mine, theirs, whole, sem) = refs[:8], refs[8:]
    for i, piece in enumerate(maps):
        pltpu.make_async_copy(piece, whole.at[pl.ds(i * 64, 64)], sem.at[0]).start()
    spread = matching(128, 16, 512, 16)
    lane = lax.broadcasted_iota(jnp.int32, (1, 512), 1)
    first = jnp.zeros((1, 512), jnp.int32)
    for i in range(8):
        first = jnp.where(lane >> 6 == i, map_slots[i], first)
    lane_slot = first + ((lane >> 4) & 3)
    pltpu.make_async_copy(whole, whole, sem.at[0]).wait()
    chosen = []
    for t in range(2):
        down = ints[ROW_BLOCKS.index(8 * t)].T
        place = lanes(128, 16, 1) == down[:, 7:8] >> 3
        own = kept(lanes(128, 128, 16) == down[:, 4:5], dot(place.astype(jnp.bfloat16), ranks[t]))
        chosen.append(kept(lane_slot == down[:, 0:1], dot(own, spread)))
    chosen = jnp.concatenate(chosen, axis=0)
    columns = whole.shape[1] // 4

    def chunk(i, carry):
        part = pl.ds(pl.multiple_of(i * columns, 128), columns)
        both = dot(chosen, whole[:, part]).astype(jnp.bfloat16)
        mine[:, part] = both[:128]
        theirs[:, part] = both[128:]
        return carry

    lax.fori_loop(0, 4, chunk, 0)


def weight_blocks(shard, ci):
    other = send(shard, OTHER_ROLE)
    same = jnp.where(ci == 0, shard, send(shard, SAME_ROLE))
    same_low, other_high = send(same, X_UP), send(other, X_DOWN)
    other_low, same_high = send(other, X_UP), send(same, X_DOWN)
    same_far, other_far = send(same_low, X_UP), send(other_high, X_DOWN)
    return [same, same_low, same_high, same_far, other, other_low, other_high, other_far]


def local(
    hidden_states,
    norm_gain,
    gate_base,
    up_base,
    down_base,
    shrink_gu,
    expand_gu,
    down_shrink_maps,
    down_expand_maps,
    token_adapter,
    adapter_slot,
):
    xi, ci, yi, hi, li = (lax.axis_index(name) for name in ALL)
    own_count, width = hidden_states.shape
    units = gate_base.shape[1]
    adapter_list = adapter_slot.shape[0]
    owner_partial = adapter_list // 16
    total = 16 * own_count

    slab_at = [((xi + dx) % 4) * 2 + (ci if half == 0 else 1 - ci) for half in range(2) for dx in X_ORDER]

    slab_at = jnp.stack(slab_at).astype(jnp.int32)

    gate_up = weight_blocks(jnp.concatenate([gate_base, up_base], axis=1), ci)
    mine = [rms_normed(hidden_states, norm_gain)]
    for k in range(7):
        mine.append(send(mine[SOURCE[k]], TREE[k]))
    theirs = [send(block, CORE) for block in mine]
    shards = [(mine + theirs)[k] for k in ROW_BLOCKS]

    shrink = send(shrink_gu, OTHER_ROLE)
    expand = send(expand_gu, OTHER_ROLE)
    down = weight_blocks(down_base, ci)
    down_shrink = send(down_shrink_maps, OTHER_ROLE)
    down_expand = send(down_expand_maps, OTHER_ROLE)

    maps = [down_expand]
    for k in range(7):
        maps.append(send(maps[SOURCE[k]], TREE[k]))

    def pick(table, k):
        return jnp.where(ci == 0, table[0][k], table[1][k])

    map_slots = []
    for k in range(8):
        from_y, from_l = (yi + pick(BLOCK_Y, k)) % 4, (li + pick(BLOCK_L, k)) % 2
        map_slots.append((from_y * 4 + jnp.where(ci == 0, hi * 2 + from_l, 3 - hi * 2 - from_l)) * owner_partial)
    map_slots = jnp.stack(map_slots).astype(jnp.int32)

    half_count = total // 2
    vmem = pl.BlockSpec(memory_space=pltpu.VMEM)
    smem = pl.BlockSpec(memory_space=pltpu.SMEM)
    stay = pl.BlockSpec(memory_space=pl.ANY)

    own_adapters = token_adapter.reshape(16, own_count)
    ints = pl.pallas_call(
        place_kernel,
        out_shape=jax.ShapeDtypeStruct((16, 8, own_count), jnp.int32),
        in_specs=[smem, smem, vmem, vmem],
        out_specs=vmem,
        scratch_shapes=[pltpu.VMEM((2, 16, own_count), jnp.int32)],
        name="places",
    )(jnp.stack([ci, yi, hi, li]), adapter_slot, own_adapters, send(own_adapters, CORE))

    def ranks_of(first, last, before, out_shape):
        count = (last - first) * own_count
        return pl.pallas_call(
            functools.partial(rank_kernel, first),
            out_shape=out_shape,
            in_specs=[vmem] * 3 + [stay] * (last - first),
            out_specs=vmem,
            scratch_shapes=[
                pltpu.VMEM((64, 128), jnp.float32),
                pltpu.VMEM((count, width), jnp.bfloat16),
                pltpu.SemaphoreType.DMA((count // TILE,)),
            ],
            name="ranks",
        )(shrink, ints, before, *shards[first:last])

    nothing = jnp.zeros((256, 128), jnp.float32)
    packed = jax.ShapeDtypeStruct((64, 128), jnp.float32)
    packed = ranks_of(LATE_BLOCKS, 16, nothing, packed)
    spread = jax.ShapeDtypeStruct((16, 64, 128), jnp.bfloat16)
    spread = ranks_of(0, LATE_BLOCKS, packed, spread)
    ranks = lax.all_to_all(spread, GROUP, split_axis=0, concat_axis=0, tiled=True).reshape(1024, 128)

    def hidden_half(i, before, kind):
        return pl.pallas_call(
            functools.partial(hidden_kernel, 8 * i),
            out_shape=(jax.ShapeDtypeStruct((half_count, units), jnp.bfloat16), jax.ShapeDtypeStruct((256, 128), kind)),
            in_specs=[smem] + [vmem] * 5 + [stay] * 16,
            out_specs=(vmem, vmem),
            scratch_shapes=[
                pltpu.VMEM((256, 128), jnp.float32),
                pltpu.VMEM((half_count, width), jnp.bfloat16),
                pltpu.VMEM((width, 2 * units), jnp.bfloat16),
                pltpu.VMEM((128, 1024), jnp.bfloat16),
                pltpu.VMEM((128, 1024), jnp.bfloat16),
                pltpu.VMEM((1024, 128), jnp.bfloat16),
                pltpu.SemaphoreType.DMA((half_count // TILE,)),
                pltpu.SemaphoreType.DMA((1,)),
            ],
            name="hidden",
        )(
            slab_at,
            ranks,
            ints,
            expand,
            down_shrink,
            before,
            *shards[8 * i : 8 * i + 8],
            *gate_up,
        )

    def down_quarter(hidden, i):
        return pl.pallas_call(
            down_kernel,
            grid=(4,),
            out_shape=(jax.ShapeDtypeStruct((TILE, width), jnp.bfloat16),) * 2,
            in_specs=[smem, pl.BlockSpec((2 * TILE, units), lambda g: (i, 0))] + [stay] * 8,
            out_specs=(pl.BlockSpec((TILE, width // 4), lambda g: (0, g)),) * 2,
            scratch_shapes=[pltpu.VMEM((4, units, width // 4), jnp.bfloat16), pltpu.SemaphoreType.DMA((4,))],
            name="down",
        )(slab_at, hidden, *down)

    def add(left, right):
        return (left.astype(jnp.float32) + right.astype(jnp.float32)).astype(jnp.bfloat16)

    sums = [None] * 8
    packed_down = nothing
    for i, kind in enumerate((jnp.float32, jnp.bfloat16)):
        hidden, packed_down = hidden_half(i, packed_down, kind)
        for j in range(2):
            mine_part, theirs_part = down_quarter(hidden, j)
            swapped = send(theirs_part, CORE)
            added = [add(mine_part[at : at + 128], swapped[at : at + 128]) for at in (0, 128)]
            for k, value in zip(HALVES[i][2 * j : 2 * j + 2], lax.optimization_barrier(added)):
                sums[k] = value

    packed_down = packed_down.reshape(16, 16, 128)
    arrived = lax.all_to_all(packed_down, GROUP, split_axis=0, concat_axis=0, tiled=True)
    down_ranks = jnp.sum(arrived.astype(jnp.float32), axis=0).astype(jnp.bfloat16)
    both_ranks = jnp.stack([down_ranks, send(down_ranks, CORE)])
    own_adapter, their_adapter = pl.pallas_call(
        adapter_kernel,
        out_shape=(jax.ShapeDtypeStruct((own_count, width), jnp.bfloat16),) * 2,
        in_specs=[smem] + [vmem] * 2 + [stay] * 8,
        out_specs=(vmem, vmem),
        scratch_shapes=[pltpu.VMEM((512, width), jnp.bfloat16), pltpu.SemaphoreType.DMA((1,))],
        name="adapters",
    )(map_slots, both_ranks, ints, *maps)
    adapter_term = own_adapter.astype(jnp.float32) + send(their_adapter, CORE).astype(jnp.float32)

    for k in (6, 5, 4, 3, 2, 1):
        sums[SOURCE[k]] = add(sums[SOURCE[k]], send(sums[k + 1], TREE_BACK[k]))
    last = send(sums[1], TREE_BACK[0]).astype(jnp.float32)
    return (sums[0].astype(jnp.float32) + last + adapter_term).astype(jnp.bfloat16)


def solution(mesh):
    fine = Mesh(mesh.devices.reshape(4, 2, 4, 2, 2), ALL)
    row, col = ("x", "c"), ("y", "h", "l")
    in_specs = (
        P(row + col, None),
        P(),
        P(row, col),
        P(row, col),
        P(col, row),
        P(col, None),
        P(None, None, col),
        P(None, col),
        P(col, None),
        P(row),
        P(),
    )
    out_specs = P(row + col, None)
    return jax.shard_map(local, mesh=fine, in_specs=in_specs, out_specs=out_specs, check_vma=False)
```
